32 devices in a mesh: ens: 2 (over core), lat: 4 (over z), lon: 4 (over y, x).
Axes of the slice: x: 2, y: 2, z: 4, core: 2. Of those that a mesh axis runs over, the one named last changes fastest.
Arguments:
- grad_tokens: bfloat16 [104, 32768], P(None, ('lat', 'lon')), may hold values from -6 to 6
- token_index: int32 [64, 512], P('lat', 'lon'), may hold values from 0 to 32767, as said below
- members: bfloat16 [4, 104, 64, 512], P('ens', None, 'lat', 'lon'), may hold values from -6 to 6
- lat_taps: float32 [17], replicated, may hold values from 0.05 to 1
- lon_taps: float32 [17], replicated, may hold values from 0.05 to 1
Outputs:
- increment: float32 [104, 64, 512], P('ens', 'lat', 'lon')
The draws below stay inside these ranges and needn't reach their ends.
Inputs may be any that keep to these rules, and one draw needn't show every extreme that they name: `token_index`: every token is the token of exactly one cell. With grid blocks numbered b = (latitude block) * (longitude blocks) + (longitude block), each of 16 x 128 cells, the cells of block b that take tokens from s * 2048 .. (s + 1) * 2048 - 1 take exactly the tokens s * 2048 + b * 128 + k for k = 0 .. 127, in any order over the block's cells.
All inputs are finite; a program needn't handle non-finite values.
Results may differ from the reference program's by a relative error of at most 0.0003.
Values may be sent and summed in bfloat16 or wider, within the bound.
No kernel may reach another device: no remote copies, remote signals or barrier semaphores. Data moves between devices by JAX's collectives and lax.ppermute only.
A program may use at most 64 MiB of HBM per device.

```python
import math
import jax
import jax.numpy as jnp
from jax import lax

HALO = 8
LAT_DEV = 16
LON_DEV = 128
CHANNELS = 104
NLAT = 64
NLON = 512
TOKENS = 32768
MEMBERS = 4
TAPS = 17


def draw_token_index(key, part):
    blocks_lat = NLAT // LAT_DEV
    blocks_lon = NLON // LON_DEV
    blocks = blocks_lat * blocks_lon
    cells = LAT_DEV * LON_DEV
    piece = cells // blocks
    keys = jax.random.split(key, blocks)
    orders = jax.vmap(lambda k: jax.random.permutation(k, cells))(keys).astype(jnp.int32)
    block_ids = jnp.arange(blocks, dtype=jnp.int32)[:, None]
    source = orders // piece
    within = orders % piece
    token = source * cells + block_ids * piece + within
    token = token.reshape(blocks_lat, blocks_lon, LAT_DEV, LON_DEV)
    token = jnp.transpose(token, (0, 2, 1, 3)).reshape(NLAT, NLON)
    return token.astype(jnp.int32)


def block_scale(rng, dims, pieces, least, largest):
    loudness = 1.0
    for position, parts in pieces:
        draws = jax.random.uniform(jax.random.fold_in(jax.random.fold_in(rng, 6), position), (parts,), jnp.float32, least / len(pieces), largest / len(pieces))
        loudness = loudness * jnp.repeat(jnp.exp(draws), dims[position] // parts).reshape((-1,) + (1,) * (len(dims) - 1 - position))
    return loudness


def noise(rng, shape, scale, most, pieces=(), kind=jnp.bfloat16):
    level = block_scale(rng, shape, pieces, -0.22, 0.18) if pieces else 1.0
    entries = jax.random.normal(rng, shape, jnp.float32) * scale * level
    return jnp.minimum(jnp.maximum(entries, -most), most).astype(kind)


def setup_inputs(seed: int = 0) -> dict:
    splits = jax.random.split(jax.random.key(seed), 6)
    return {
        "grad_tokens": noise(splits[0], (CHANNELS, TOKENS), 1.0, 6.0, ((1, 16),)),
        "token_index": draw_token_index(jax.random.fold_in(splits[5], 71), 0),
        "members": noise(splits[2], (MEMBERS, CHANNELS, NLAT, NLON), 1.0, 6.0, ((0, 2), (2, 4), (3, 4))),
        "lat_taps": jnp.clip(jnp.exp(jax.random.uniform(splits[3], (TAPS,), jnp.float32, math.log(0.05), math.log(1.0))), 0.05, 1.0),
        "lon_taps": jnp.clip(jnp.exp(jax.random.uniform(splits[4], (TAPS,), jnp.float32, math.log(0.05), math.log(1.0))), 0.05, 1.0),
    }


def lat_smooth(field, taps):
    upper = jnp.arange(NLAT, dtype=jnp.int32)[:, None]
    lower = jnp.arange(NLAT, dtype=jnp.int32)[None, :]
    offset = upper - lower + HALO
    inside = (offset >= 0) & (offset <= 2 * HALO)
    matrix = jnp.where(inside, taps[jnp.clip(offset, 0, 2 * HALO)], 0.0)
    return jnp.einsum("cul,ui->cil", field, matrix, precision=lax.Precision.HIGHEST)


def lon_smooth(field, taps):
    total = jnp.zeros_like(field)
    for shift in range(-HALO, HALO + 1):
        total = total + taps[shift + HALO] * jnp.roll(field, -shift, axis=2)
    return total


def localize(field, lat_w, lon_w):
    return lon_smooth(lat_smooth(field, lat_w), lon_w)


def reference(grad_tokens, token_index, members, lat_taps, lon_taps):
    grid = jnp.take(grad_tokens, token_index.reshape(-1).astype(jnp.int32), axis=1)
    grid = grid.reshape(CHANNELS, NLAT, NLON).astype(jnp.float32)
    lat_back = lat_taps[::-1]
    lon_back = lon_taps[::-1]

    def one_member(total, member):
        member = member.astype(jnp.float32)
        control = localize(member * grid, lat_back, lon_back)
        return total + member * localize(control, lat_taps, lon_taps), None

    start = jnp.zeros((CHANNELS, NLAT, NLON), jnp.float32)
    total, _ = lax.scan(one_member, start, members)
    return total / (MEMBERS - 1)
```

```python
import functools

import jax
import jax.numpy as jnp
from jax import lax
from jax.experimental import pallas as pl
from jax.experimental.pallas import tpu as pltpu
from jax.sharding import PartitionSpec as P

LANES = 128
F32 = jnp.float32
BF16 = jnp.bfloat16


def dot(a, b):
    return lax.dot_general(a, b, (((1,), (0,)), ((), ())), preferred_element_type=F32)


def split(v):
    hi = v.astype(BF16)
    return hi, (v - hi.astype(F32)).astype(BF16)


def split_outside(v):
    hi = lax.reduce_precision(v, 8, 7)
    return hi.astype(BF16), (v - hi).astype(BF16)


def band(taps, offset):
    total = jnp.zeros(offset.shape, F32)
    for k in range(taps.shape[0]):
        total = total + jnp.where(offset == k, taps[k], 0.0)
    return total


def lon_matrix(taps, cols, strip):
    count = taps.shape[0]
    radius2 = count - 1
    longer = jnp.concatenate([jnp.zeros(radius2, F32), taps, jnp.zeros(radius2, F32)])
    both = jnp.stack(
        [jnp.sum(taps * longer[radius2 - d : radius2 - d + count]) for d in range(-radius2, radius2 + 1)]
    )
    place = jnp.arange(2 * LANES, dtype=jnp.int32)[:, None]
    inner = place % strip
    source = jnp.where(
        place < cols,
        place,
        jnp.where(place < cols + LANES // 2, inner - strip, cols + inner),
    )
    target = jnp.arange(cols, dtype=jnp.int32)[None, :]
    matrix = band(both, source - target + radius2)
    hi, lo = split_outside(matrix)
    return jnp.concatenate([hi, lo], axis=1)


def lat_matrix(taps, rows, lat_pos, lat_count):
    radius = (taps.shape[0] - 1) // 2
    out_row = jnp.arange(3 * rows, dtype=jnp.int32)[:, None] - rows
    mid_row = jnp.arange(rows + 2 * radius, dtype=jnp.int32) - radius
    own_row = jnp.arange(rows, dtype=jnp.int32)[None, :]
    whole_row = lat_pos * rows + mid_row
    inside = (whole_row >= 0) & (whole_row < lat_count * rows)
    spread = band(taps, mid_row[None, :] - out_row + radius)
    gather = band(taps[::-1], own_row - mid_row[:, None] + radius)
    gather = jnp.where(inside[:, None], gather, 0.0)
    matrix = jnp.sum(spread[:, :, None] * gather[None, :, :], axis=1)
    hi, lo = split_outside(matrix)
    return jnp.concatenate([hi, lo, hi], axis=1)


def pick_matrix(slot, strip, cols):
    lane = lax.broadcasted_iota(jnp.int32, (cols, LANES), 1)
    row = lax.broadcasted_iota(jnp.int32, (cols, LANES), 0)
    here = lane // strip == slot
    first = here & (row == lane % strip)
    last = here & (row == cols - strip + lane % strip)
    one = jnp.concatenate([first.astype(F32), last.astype(F32)], axis=1)
    return one.astype(BF16)


def pack_kernel(strip, slots, w_ref, first_ref, last_ref):
    members, channels, rows, cols = w_ref.shape
    per = max(1, slots // members)
    for h in range(max(1, members // slots)):
        total = None
        for k in range(slots):
            c2, m = (k // members, k % members) if members <= slots else (0, h * slots + k)
            plane = w_ref[m].reshape(channels // per, per, rows, cols)[:, c2]
            part = dot(plane.reshape(-1, cols), pick_matrix(k, strip, cols))
            total = part if total is None else total + part
        total = total.astype(BF16)
        first_ref[h] = total[:, :LANES].reshape(channels // per, rows, LANES)
        last_ref[h] = total[:, LANES:].reshape(channels // per, rows, LANES)


def gather_kernel(strip, slots, moved_ref, offset_ref, grid_ref, first_ref, last_ref, scratch):
    pieces, channels, width = moved_ref.shape
    rows, cols = offset_ref.shape
    scratch[channels:] = jnp.zeros((scratch.shape[0] - channels, rows, cols), F32)
    tokens = jnp.concatenate([moved_ref[n] for n in range(pieces)], axis=1)
    token = lax.broadcasted_iota(jnp.int32, (pieces * width, 2 * cols), 0)
    for i in range(0, rows, 2):
        wanted = jnp.concatenate([offset_ref[i : i + 1], offset_ref[i + 1 : i + 2]], axis=1)
        chosen = jnp.where(token == wanted, 1.0, 0.0).astype(BF16)
        found = dot(tokens, chosen)
        scratch[:channels, i, :] = found[:, :cols]
        scratch[:channels, i + 1, :] = found[:, cols:]
    grid = scratch[...].astype(BF16)
    grid_ref[...] = grid[:channels]
    groups = scratch.shape[0] // slots
    planes = grid.reshape(groups, slots, rows, cols)
    total = None
    for k in range(slots):
        part = dot(planes[:, k].reshape(-1, cols), pick_matrix(k, strip, cols))
        total = part if total is None else total + part
    total = total.astype(BF16)
    first_ref[...] = total[:, :LANES].reshape(groups, rows, LANES)
    last_ref[...] = total[:, LANES:].reshape(groups, rows, LANES)


def smooth_kernel(
    strip, slots, start, count, own_ref, up_ref, down_ref, left_ref, right_ref,
    grid_ref, grid_left_ref, grid_right_ref, lon_ref, lat_ref, out_ref, out_up_ref, out_down_ref,
):
    members, channels, rows, cols = own_ref.shape
    per = max(1, slots // members)
    lon_both = lon_ref[...]
    lon_hi = lon_both[:, :cols]
    lat = lat_ref[...]
    lane = lax.broadcasted_iota(jnp.int32, (rows, LANES), 1)
    half = LANES // 2
    src = lax.broadcasted_iota(jnp.int32, (LANES, LANES), 0)
    dst = lax.broadcasted_iota(jnp.int32, (LANES, LANES), 1)
    dst_slot = dst // strip
    dst_channel = dst_slot // members if members <= slots else jnp.zeros_like(dst)
    low = lane < half
    slot_of = (lane % half) // strip

    def body(step, carry):
        group = start // per + step
        first = group * per
        expand = src == ((first + dst_channel) % slots) * strip + dst % strip
        expand = expand.astype(F32).astype(BF16)
        grid_left = dot(grid_left_ref[first // slots], expand)
        grid_right = dot(grid_right_ref[first // slots], expand)
        grids = [grid_ref[first + c].astype(F32) for c in range(per)]
        outs = [[None] * 3 for _ in range(per)]
        for h in range(max(1, members // slots)):
            left = left_ref[h, group].astype(F32) * grid_left
            right = right_ref[h, group].astype(F32) * grid_right
            sides = (
                split(jnp.where(low, left, pltpu.roll(right, half, 1))),
                split(jnp.where(low, pltpu.roll(left, half, 1), right)),
            )
            parts = ([], [])
            where = []
            for k in range(slots):
                c, m = (k // members, k % members) if members <= slots else (0, h * slots + k)
                where.append((c, m))
                mine = split(own_ref[m, first + c].astype(F32) * grids[c])
                side = sides[k * 2 // slots]
                keep = slot_of == k % (slots // 2)
                for p in range(2):
                    edge = jnp.where(keep, side[p], jnp.zeros_like(side[p]))
                    parts[p].append(jnp.concatenate([mine[p], edge], axis=1))
            big = dot(jnp.concatenate(parts[0], axis=0), lon_both)
            small = dot(jnp.concatenate(parts[1], axis=0), lon_hi)
            smoothed = big[:, :cols] + big[:, cols:] + small
            hi, lo = split(smoothed)
            stack = []
            for k in range(slots):
                a, b = hi[k * rows : (k + 1) * rows], lo[k * rows : (k + 1) * rows]
                stack.append(jnp.concatenate([a, a, b], axis=0))
            spread = dot(lat, jnp.concatenate(stack, axis=1))
            for k, (c, m) in enumerate(where):
                for r, ref in enumerate((up_ref, own_ref, down_ref)):
                    piece = spread[r * rows : (r + 1) * rows, k * cols : (k + 1) * cols]
                    term = piece * ref[m, first + c].astype(F32)
                    outs[c][r] = term if outs[c][r] is None else outs[c][r] + term
        for c in range(per):
            at = step * per + c
            out_up_ref[at] = outs[c][0]
            out_ref[at] = outs[c][1]
            out_down_ref[at] = outs[c][2]
        return carry

    lax.fori_loop(0, count // per, body, 0)


def whole(n):
    return [pl.BlockSpec(memory_space=pltpu.VMEM)] * n


def local(chunks, grad_tokens, token_index, members, lat_taps, lon_taps):
    ens, lat_count, lon_count = (lax.axis_size(a) for a in ("ens", "lat", "lon"))
    ens_pos, lat_pos, lon_pos = (lax.axis_index(a) for a in ("ens", "lat", "lon"))
    channels, cells = grad_tokens.shape
    rows, cols = token_index.shape
    own_channels = channels // ens
    blocks = lat_count * lon_count
    piece = cells // blocks
    strip = lon_taps.shape[0] - 1
    slots = LANES // strip
    assert cols == LANES and lat_taps.shape[0] - 1 <= rows

    tokens = lax.dynamic_slice_in_dim(grad_tokens, ens_pos * own_channels, own_channels, 0)
    tokens = tokens.reshape(own_channels, blocks, piece).transpose(1, 0, 2)
    moved = lax.all_to_all(tokens, ("lat", "lon"), split_axis=0, concat_axis=0, tiled=True)
    if piece != LANES:
        moved = moved.transpose(1, 0, 2).reshape(own_channels, cells // LANES, LANES).transpose(1, 0, 2)
    block_id = lat_pos * lon_count + lon_pos
    offset = (token_index // cells) * piece + token_index % cells - block_id * piece

    if ens == 2:
        given = lax.dynamic_slice_in_dim(members, (1 - ens_pos) * own_channels, own_channels, 1)
        kept = lax.dynamic_slice_in_dim(members, ens_pos * own_channels, own_channels, 1)
        taken = lax.ppermute(given, "ens", [(0, 1), (1, 0)])
        w = jnp.concatenate([kept, taken], axis=0)
    else:
        w = lax.all_to_all(members, "ens", split_axis=1, concat_axis=0, tiled=True)
    count = w.shape[0]
    per = max(1, slots // count)
    parts = max(1, count // slots)

    to_down = [(i, i + 1) for i in range(lat_count - 1)]
    to_up = [(i + 1, i) for i in range(lat_count - 1)]
    to_right = [(i, (i + 1) % lon_count) for i in range(lon_count)]
    to_left = [((i + 1) % lon_count, i) for i in range(lon_count)]
    w_up = lax.ppermute(w, "lat", to_down)
    w_down = lax.ppermute(w, "lat", to_up)

    strips = jax.ShapeDtypeStruct((parts, own_channels // per, rows, LANES), BF16)
    w_first, w_last = pl.pallas_call(
        functools.partial(pack_kernel, strip, slots),
        out_shape=(strips, strips), in_specs=whole(1), out_specs=whole(2), name="pack",
    )(w)
    w_left = lax.ppermute(w_last, "lon", to_right)
    w_right = lax.ppermute(w_first, "lon", to_left)

    lon_both = lon_matrix(lon_taps, cols, strip)
    lat = lat_matrix(lat_taps, rows, lat_pos, lat_count)

    padded = -(-own_channels // slots) * slots
    edges = jax.ShapeDtypeStruct((padded // slots, rows, LANES), BF16)
    grid, g_first, g_last = pl.pallas_call(
        functools.partial(gather_kernel, strip, slots),
        out_shape=(jax.ShapeDtypeStruct((own_channels, rows, cols), BF16), edges, edges),
        in_specs=whole(2), out_specs=whole(3),
        scratch_shapes=[pltpu.VMEM((padded, rows, cols), F32)], name="gather",
    )(moved, offset)
    g_left = lax.ppermute(g_last, "lon", to_right)
    g_right = lax.ppermute(g_first, "lon", to_left)

    chunks = chunks if own_channels % (chunks * per) == 0 else 1
    size = own_channels // chunks
    block = jax.ShapeDtypeStruct((size, rows, cols), F32)
    outs = []
    for n in range(chunks):
        own, up, down = pl.pallas_call(
            functools.partial(smooth_kernel, strip, slots, n * size, size),
            out_shape=(block,) * 3, in_specs=whole(10), out_specs=whole(3), name=f"smooth{n}",
        )(w, w_up, w_down, w_left, w_right, grid, g_left, g_right, lon_both, lat)
        from_up = lax.ppermute(down, "lat", to_down)
        from_down = lax.ppermute(up, "lat", to_up)
        outs.append((own + from_up + from_down) / (count - 1))
    return jnp.concatenate(outs, axis=0) if chunks > 1 else outs[0]


def solution(mesh):
    in_specs = (P(None, ("lat", "lon")), P("lat", "lon"), P("ens", None, "lat", "lon"), P(), P())
    out_specs = P("ens", "lat", "lon")
    return jax.shard_map(
        functools.partial(local, 2), mesh=mesh, in_specs=in_specs, out_specs=out_specs, check_vma=False
    )
```

```python
import functools

import jax
import jax.numpy as jnp
from jax import lax
from jax.experimental import pallas as pl
from jax.experimental.pallas import tpu as pltpu
from jax.sharding import PartitionSpec as P

LANES = 128
F32 = jnp.float32
BF16 = jnp.bfloat16
UNIT = 7
GRANT = 24 << 20


def dot(a, b):
    return lax.dot_general(a, b, (((1,), (0,)), ((), ())), preferred_element_type=F32)


def split(v):
    hi = v.astype(BF16)
    return hi, (v - hi.astype(F32)).astype(BF16)


def band(taps, offset):
    total = jnp.zeros(offset.shape, F32)
    for k, tap in enumerate(taps):
        total = jnp.where(offset == k, tap, total)
    return total


def matrix_kernel(strip, lat_count, lat_taps_ref, lon_taps_ref, lon_ref, lat_ref):
    cols, rows = lon_ref.shape[1] // 2, lat_ref.shape[0] // 3
    count = lon_taps_ref.shape[0]
    iota = lax.broadcasted_iota
    taps = [lon_taps_ref[k] for k in range(count)]
    half = [sum(taps[a] * taps[a - d] for a in range(d, count)) for d in range(count)]
    both = half[:0:-1] + half
    place = iota(jnp.int32, (2 * LANES, cols), 0)
    inner = place % strip
    source = jnp.where(
        place < cols, place, jnp.where(place < cols + LANES // 2, inner - strip, cols + inner)
    )
    hi, lo = split(band(both, source - iota(jnp.int32, (2 * LANES, cols), 1) + count - 1))
    lon_ref[...] = jnp.concatenate([hi, lo], axis=1)
    count = lat_taps_ref.shape[0]
    radius = (count - 1) // 2
    taps = [lat_taps_ref[k] for k in range(count)]
    middle = rows + 2 * radius
    out_row = iota(jnp.int32, (3 * rows, middle), 0) - rows
    mid_row = iota(jnp.int32, (3 * rows, middle), 1) - radius
    spread = band(taps, mid_row - out_row + radius)
    mid_row = iota(jnp.int32, (middle, rows), 0) - radius
    gather = band(taps[::-1], iota(jnp.int32, (middle, rows), 1) - mid_row + radius)
    whole_row = lax.axis_index("lat") * rows + mid_row
    gather = jnp.where((whole_row >= 0) & (whole_row < lat_count * rows), gather, 0.0)
    hi, lo = split(jnp.dot(spread, gather, precision=lax.Precision.HIGHEST, preferred_element_type=F32))
    lat_ref[...] = jnp.concatenate([hi, lo, hi], axis=1)


def pick_matrix(slot, strip, cols):
    lane = lax.broadcasted_iota(jnp.int32, (cols, LANES), 1)
    row = lax.broadcasted_iota(jnp.int32, (cols, LANES), 0)
    here = lane // strip == slot
    first = here & (row == lane % strip)
    last = here & (row == cols - strip + lane % strip)
    one = jnp.concatenate([first.astype(F32), last.astype(F32)], axis=1)
    return one.astype(BF16)


def pack_kernel(strip, slots, w_ref, first_ref, last_ref):
    members, channels, rows, cols = w_ref.shape
    per = max(1, slots // members)
    for h in range(max(1, members // slots)):
        total = None
        for k in range(slots):
            c2, m = (k // members, k % members) if members <= slots else (0, h * slots + k)
            plane = w_ref[m].reshape(channels // per, per, rows, cols)[:, c2]
            part = dot(plane.reshape(-1, cols), pick_matrix(k, strip, cols))
            total = part if total is None else total + part
        total = total.astype(BF16)
        first_ref[h] = total[:, :LANES].reshape(channels // per, rows, LANES)
        last_ref[h] = total[:, LANES:].reshape(channels // per, rows, LANES)


def gather_kernel(strip, slots, moved_ref, offset_ref, grid_ref, first_ref, last_ref, scratch):
    pieces, channels, width = moved_ref.shape
    rows, cols = offset_ref.shape
    scratch[channels:] = jnp.zeros((scratch.shape[0] - channels, rows, cols), F32)
    tokens = jnp.concatenate([moved_ref[n] for n in range(pieces)], axis=1)
    token = lax.broadcasted_iota(jnp.int32, (pieces * width, 2 * cols), 0)
    for i in range(0, rows, 2):
        wanted = jnp.concatenate([offset_ref[i : i + 1], offset_ref[i + 1 : i + 2]], axis=1)
        chosen = jnp.where(token == wanted, 1.0, 0.0).astype(BF16)
        found = dot(tokens, chosen)
        scratch[:channels, i, :] = found[:, :cols]
        scratch[:channels, i + 1, :] = found[:, cols:]
    grid = scratch[...].astype(BF16)
    grid_ref[...] = grid[:channels]
    groups = scratch.shape[0] // slots
    planes = grid.reshape(groups, slots, rows, cols)
    total = None
    for k in range(slots):
        part = dot(planes[:, k].reshape(-1, cols), pick_matrix(k, strip, cols))
        total = part if total is None else total + part
    total = total.astype(BF16)
    first_ref[...] = total[:, :LANES].reshape(groups, rows, LANES)
    last_ref[...] = total[:, LANES:].reshape(groups, rows, LANES)


def smooth_kernel(
    strip, slots, start, unit, own_ref, up_ref, down_ref, left_ref, right_ref,
    grid_ref, grid_left_ref, grid_right_ref, lon_ref, lat_ref, out_up_ref, out_ref, out_down_ref,
    hi_ref, lo_ref, mid_ref,
):
    members, channels, rows, cols = own_ref.shape
    per, parts = max(1, slots // members), max(1, members // slots)
    groups = out_ref.shape[0] // per * parts
    half = LANES // 2
    height = slots * rows
    src = lax.broadcasted_iota(jnp.int32, (LANES, LANES), 0)
    dst = lax.broadcasted_iota(jnp.int32, (LANES, LANES), 1)
    lane = lax.broadcasted_iota(jnp.int32, (rows, LANES), 1)
    low = lane < half
    slot_of = (lane % half) // strip

    def place(n):
        first, h = start + n // parts * per, n % parts
        where = [(k // members, k % members) if parts == 1 else (0, h * slots + k) for k in range(slots)]
        return first, h, where

    def weigh(n):
        first, h, where = place(n)
        dst_channel = dst // strip // members if parts == 1 else jnp.zeros_like(dst)
        expand = src == ((first + dst_channel) % slots) * strip + dst % strip
        expand = jnp.where(expand, 1.0, 0.0).astype(BF16)
        left = left_ref[h, first // per].astype(F32) * dot(grid_left_ref[first // slots], expand)
        right = right_ref[h, first // per].astype(F32) * dot(grid_right_ref[first // slots], expand)
        sides = (
            split(jnp.where(low, left, pltpu.roll(right, half, 1))),
            split(jnp.where(low, pltpu.roll(left, half, 1), right)),
        )
        for k, (c, m) in enumerate(where):
            mine = split(own_ref[m, first + c].astype(F32) * grid_ref[first + c].astype(F32))
            side = sides[k * 2 // slots]
            keep = slot_of == k % (slots // 2)
            at = pl.ds(n * height + k * rows, rows)
            for p, ref in enumerate((hi_ref, lo_ref)):
                ref[at, :cols] = mine[p]
                ref[at, cols:] = jnp.where(keep, side[p], jnp.zeros_like(side[p]))

    def along_lon(n, many):
        at = pl.ds(n * height, many * height)
        big = dot(hi_ref[at, :], lon_ref[...])
        small = dot(lo_ref[at, :], lon_ref[:, :cols])
        hi, lo = split(big[:, :cols] + big[:, cols:] + small)
        for k in range(many * slots):
            to = pl.ds((n * slots + k) * cols, cols)
            rest = slice(k * rows, (k + 1) * rows)
            mid_ref[:rows, to] = hi[rest]
            mid_ref[rows : 2 * rows, to] = hi[rest]
            mid_ref[2 * rows :, to] = lo[rest]

    def along_lat(n):
        first, h, where = place(n)
        spread = dot(lat_ref[...], mid_ref[:, pl.ds(n * slots * cols, slots * cols)])
        for r, (ref, out) in enumerate(((up_ref, out_up_ref), (own_ref, out_ref), (down_ref, out_down_ref))):
            sums = {}
            for k, (c, m) in enumerate(where):
                piece = spread[r * rows : (r + 1) * rows, k * cols : (k + 1) * cols]
                term = piece * ref[m, first + c].astype(F32)
                sums[c] = sums[c] + term if c in sums else term
            for c, total in sums.items():
                at = first - start + c
                out[at] = total if h == 0 else out[at] + total

    units = [range(n, min(n + unit, groups)) for n in range(0, groups, unit)]
    for n in range(len(units) + 2):
        if n < len(units):
            for g in units[n]:
                weigh(g)
        if 0 <= n - 1 < len(units):
            along_lon(units[n - 1][0], len(units[n - 1]))
        if 0 <= n - 2:
            for g in units[n - 2]:
                along_lat(g)


def whole(n):
    return [pl.BlockSpec(memory_space=pltpu.VMEM)] * n


def smooth_call(strip, slots, members, rows, cols, start, size, unit=UNIT):
    block = jax.ShapeDtypeStruct((size, rows, cols), F32)
    planes = size * members
    return pl.pallas_call(
        functools.partial(smooth_kernel, strip, slots, start, unit),
        out_shape=(block,) * 3, in_specs=whole(10), out_specs=whole(3), name=f"smooth{start}",
        scratch_shapes=[
            pltpu.VMEM((planes * rows, cols + LANES), BF16),
            pltpu.VMEM((planes * rows, cols + LANES), BF16),
            pltpu.VMEM((3 * rows, planes * cols), BF16),
        ],
        compiler_params=pltpu.CompilerParams(vmem_limit_bytes=GRANT),
    )


def local(chunks, grad_tokens, token_index, members, lat_taps, lon_taps):
    ens, lat_count, lon_count = (lax.axis_size(a) for a in ("ens", "lat", "lon"))
    ens_pos, lat_pos, lon_pos = (lax.axis_index(a) for a in ("ens", "lat", "lon"))
    channels, cells = grad_tokens.shape
    rows, cols = token_index.shape
    own_channels = channels // ens
    blocks = lat_count * lon_count
    piece = cells // blocks
    strip = lon_taps.shape[0] - 1
    slots = LANES // strip
    assert cols == LANES and lat_taps.shape[0] - 1 <= rows

    tokens = lax.dynamic_slice_in_dim(grad_tokens, ens_pos * own_channels, own_channels, 0)
    tokens = tokens.reshape(own_channels, blocks, piece).transpose(1, 0, 2)
    moved = lax.all_to_all(tokens, ("lat", "lon"), split_axis=0, concat_axis=0, tiled=True)
    if piece != LANES:
        moved = moved.transpose(1, 0, 2).reshape(own_channels, cells // LANES, LANES).transpose(1, 0, 2)
    block_id = lat_pos * lon_count + lon_pos
    offset = (token_index // cells) * piece + token_index % cells - block_id * piece

    if ens == 2:
        given = lax.dynamic_slice_in_dim(members, (1 - ens_pos) * own_channels, own_channels, 1)
        kept = lax.dynamic_slice_in_dim(members, ens_pos * own_channels, own_channels, 1)
        taken = lax.ppermute(given, "ens", [(0, 1), (1, 0)])
        w = jnp.concatenate([kept, taken], axis=0)
    else:
        w = lax.all_to_all(members, "ens", split_axis=1, concat_axis=0, tiled=True)
    count = w.shape[0]
    per = max(1, slots // count)
    parts = max(1, count // slots)

    to_down = [(i, i + 1) for i in range(lat_count - 1)]
    to_up = [(i + 1, i) for i in range(lat_count - 1)]
    to_right = [(i, (i + 1) % lon_count) for i in range(lon_count)]
    to_left = [((i + 1) % lon_count, i) for i in range(lon_count)]
    w_up = lax.ppermute(w, "lat", to_down)
    w_down = lax.ppermute(w, "lat", to_up)

    strips = jax.ShapeDtypeStruct((parts, own_channels // per, rows, LANES), BF16)
    w_first, w_last = pl.pallas_call(
        functools.partial(pack_kernel, strip, slots),
        out_shape=(strips, strips), in_specs=whole(1), out_specs=whole(2), name="pack",
        compiler_params=pltpu.CompilerParams(vmem_limit_bytes=GRANT),
    )(w)
    w_left = lax.ppermute(w_last, "lon", to_right)
    w_right = lax.ppermute(w_first, "lon", to_left)

    lon_both, lat = pl.pallas_call(
        functools.partial(matrix_kernel, strip, lat_count),
        out_shape=(
            jax.ShapeDtypeStruct((2 * LANES, 2 * cols), BF16),
            jax.ShapeDtypeStruct((3 * rows, 3 * rows), BF16),
        ),
        in_specs=[pl.BlockSpec(memory_space=pltpu.SMEM)] * 2, out_specs=whole(2), name="matrices",
        compiler_params=pltpu.CompilerParams(vmem_limit_bytes=GRANT),
    )(lat_taps, lon_taps)

    padded = -(-own_channels // slots) * slots
    edges = jax.ShapeDtypeStruct((padded // slots, rows, LANES), BF16)
    grid, g_first, g_last = pl.pallas_call(
        functools.partial(gather_kernel, strip, slots),
        out_shape=(jax.ShapeDtypeStruct((own_channels, rows, cols), BF16), edges, edges),
        in_specs=whole(2), out_specs=whole(3),
        scratch_shapes=[pltpu.VMEM((padded, rows, cols), F32)], name="gather",
        compiler_params=pltpu.CompilerParams(vmem_limit_bytes=GRANT),
    )(moved, offset)
    g_left = lax.ppermute(g_last, "lon", to_right)
    g_right = lax.ppermute(g_first, "lon", to_left)

    chunks = chunks if own_channels % (chunks * per) == 0 else 1
    size = own_channels // chunks
    smooth = functools.partial(smooth_call, strip, slots, count, rows, cols)
    outs = []
    for n in range(chunks):
        up, own, down = smooth(n * size, size)(w, w_up, w_down, w_left, w_right, grid, g_left, g_right, lon_both, lat)
        from_up = lax.ppermute(down, "lat", to_down)
        from_down = lax.ppermute(up, "lat", to_up)
        outs.append((own + from_up + from_down) / (count - 1))
    return jnp.concatenate(outs, axis=0) if chunks > 1 else outs[0]


def solution(mesh):
    in_specs = (P(None, ("lat", "lon")), P("lat", "lon"), P("ens", None, "lat", "lon"), P(), P())
    out_specs = P("ens", "lat", "lon")
    return jax.shard_map(
        functools.partial(local, 2), mesh=mesh, in_specs=in_specs, out_specs=out_specs, check_vma=False
    )
```

```python
import functools

import jax
import jax.numpy as jnp
from jax import lax
from jax.experimental import pallas as pl
from jax.experimental.pallas import tpu as pltpu
from jax.sharding import PartitionSpec as P


LANES = 128
F32 = jnp.float32
BF16 = jnp.bfloat16
UNIT = 7
GRANT = 24 << 20


def dot(a, b):
    return lax.dot_general(a, b, (((1,), (0,)), ((), ())), preferred_element_type=F32)


def split(v):
    hi = v.astype(BF16)
    return hi, (v - hi.astype(F32)).astype(BF16)


def band(taps, offset):
    total = jnp.zeros(offset.shape, F32)
    for k, tap in enumerate(taps):
        total = jnp.where(offset == k, tap, total)
    return total


def fill_matrices(strip, lat_count, lat_taps_ref, lon_taps_ref, lon_ref, lat_ref):
    cols, rows = lon_ref.shape[1] // 2, lat_ref.shape[0] // 3
    count = lon_taps_ref.shape[0]
    iota = lax.broadcasted_iota
    taps = [lon_taps_ref[k] for k in range(count)]
    half = [sum(taps[a] * taps[a - d] for a in range(d, count)) for d in range(count)]
    both = half[:0:-1] + half
    place = iota(jnp.int32, (2 * LANES, cols), 0)
    inner = place % strip
    even = lax.rem(lax.axis_index("lon"), 2) == 0
    after = (place < cols + LANES // 2) == even
    source = jnp.where(place < cols, place, jnp.where(after, cols + inner, inner - strip))
    hi, lo = split(band(both, source - iota(jnp.int32, (2 * LANES, cols), 1) + count - 1))
    lon_ref[...] = jnp.concatenate([hi, lo], axis=1)
    count = lat_taps_ref.shape[0]
    radius = (count - 1) // 2
    taps = [lat_taps_ref[k] for k in range(count)]
    middle = rows + 2 * radius
    toward = jnp.where(lax.rem(lax.axis_index("lat"), 2) == 0, rows, -rows)
    place = iota(jnp.int32, (3 * rows, middle), 0)
    out_row = place % rows + (1 - place // rows) * toward
    mid_row = iota(jnp.int32, (3 * rows, middle), 1) - radius
    spread = band(taps, mid_row - out_row + radius)
    mid_row = iota(jnp.int32, (middle, rows), 0) - radius
    gather = band(taps[::-1], iota(jnp.int32, (middle, rows), 1) - mid_row + radius)
    whole_row = lax.axis_index("lat") * rows + mid_row
    gather = jnp.where((whole_row >= 0) & (whole_row < lat_count * rows), gather, 0.0)
    hi, lo = split(jnp.dot(spread, gather, precision=lax.Precision.HIGHEST, preferred_element_type=F32))
    lat_ref[...] = jnp.concatenate([hi, lo, hi], axis=1)


def pick_matrix(slot, strip, cols):
    even = lax.rem(lax.axis_index("lon"), 2) == 0
    last = cols - strip
    lane = lax.broadcasted_iota(jnp.int32, (cols, 2 * LANES), 1)
    row = lax.broadcasted_iota(jnp.int32, (cols, 2 * LANES), 0)
    first = jnp.where((lane < LANES) == even, last, 0)
    chosen = (lane % LANES // strip == slot) & (row == first + lane % strip)
    return jnp.where(chosen, 1.0, 0.0).astype(BF16)


def prepare_kernel(strip, slots, lat_count, parts, *refs):
    w_refs, (lat_taps_ref, lon_taps_ref, a_ref, b_ref, lon_ref, lat_ref) = refs[:parts], refs[parts:]
    fill_matrices(strip, lat_count, lat_taps_ref, lon_taps_ref, lon_ref, lat_ref)
    each, channels, rows, cols = w_refs[0].shape
    members = each * parts
    per = max(1, slots // members)
    for h in range(max(1, members // slots)):
        total = None
        for k in range(slots):
            c2, m = (k // members, k % members) if members <= slots else (0, h * slots + k)
            plane = w_refs[m // each][m % each].reshape(channels // per, per, rows, cols)[:, c2]
            part = dot(plane.reshape(-1, cols), pick_matrix(k, strip, cols))
            total = part if total is None else total + part
        total = total.astype(BF16)
        a_ref[h] = total[:, :LANES].reshape(channels // per, rows, LANES)
        b_ref[h] = total[:, LANES:].reshape(channels // per, rows, LANES)


def gather_kernel(strip, slots, moved_ref, offset_ref, grid_ref, a_ref, b_ref, scratch):
    pieces, channels, width = moved_ref.shape
    rows, cols = offset_ref.shape
    scratch[channels:] = jnp.zeros((scratch.shape[0] - channels, rows, cols), F32)
    tokens = jnp.concatenate([moved_ref[n] for n in range(pieces)], axis=1)
    token = lax.broadcasted_iota(jnp.int32, (pieces * width, 2 * cols), 0)
    for i in range(0, rows, 2):
        wanted = jnp.concatenate([offset_ref[i : i + 1], offset_ref[i + 1 : i + 2]], axis=1)
        chosen = jnp.where(token == wanted, 1.0, 0.0).astype(BF16)
        found = dot(tokens, chosen)
        scratch[:channels, i, :] = found[:, :cols]
        scratch[:channels, i + 1, :] = found[:, cols:]
    grid = scratch[...].astype(BF16)
    grid_ref[...] = grid[:channels]
    groups = scratch.shape[0] // slots
    planes = grid.reshape(groups, slots, rows, cols)
    total = None
    for k in range(slots):
        part = dot(planes[:, k].reshape(-1, cols), pick_matrix(k, strip, cols))
        total = part if total is None else total + part
    total = total.astype(BF16)
    a_ref[...] = total[:, :LANES].reshape(groups, rows, LANES)
    b_ref[...] = total[:, LANES:].reshape(groups, rows, LANES)


def smooth_kernel(strip, slots, start, unit, parts, *refs):
    own_refs, a_refs, b_refs = (refs[n * parts : (n + 1) * parts] for n in range(3))
    (strip_a_ref, strip_b_ref, grid_ref, grid_a_ref, grid_b_ref, lon_ref, lat_ref) = refs[3 * parts : 3 * parts + 7]
    out_a_ref, out_ref, out_b_ref, hi_ref, lo_ref, mid_ref = refs[3 * parts + 7 :]
    each, _, rows, cols = own_refs[0].shape
    members = each * parts

    def member(refs, m, c):
        return refs[m // each][m % each, c].astype(F32)

    per, folds = max(1, slots // members), max(1, members // slots)
    groups = out_ref.shape[0] // per * folds
    half = LANES // 2
    height = slots * rows
    src = lax.broadcasted_iota(jnp.int32, (LANES, LANES), 0)
    dst = lax.broadcasted_iota(jnp.int32, (LANES, LANES), 1)
    lane = lax.broadcasted_iota(jnp.int32, (rows, LANES), 1)
    low = lane < half
    slot_of = (lane % half) // strip

    def place(n):
        first, h = start + n // folds * per, n % folds
        where = [(k // members, k % members) if folds == 1 else (0, h * slots + k) for k in range(slots)]
        return first, h, where

    def weigh(n):
        first, h, where = place(n)
        dst_channel = dst // strip // members if folds == 1 else jnp.zeros_like(dst)
        expand = src == ((first + dst_channel) % slots) * strip + dst % strip
        expand = jnp.where(expand, 1.0, 0.0).astype(BF16)
        edge_a = strip_a_ref[h, first // per].astype(F32) * dot(grid_a_ref[first // slots], expand)
        edge_b = strip_b_ref[h, first // per].astype(F32) * dot(grid_b_ref[first // slots], expand)
        sides = (
            split(jnp.where(low, edge_a, pltpu.roll(edge_b, half, 1))),
            split(jnp.where(low, pltpu.roll(edge_a, half, 1), edge_b)),
        )
        for k, (c, m) in enumerate(where):
            mine = split(member(own_refs, m, first + c) * grid_ref[first + c].astype(F32))
            side = sides[k * 2 // slots]
            keep = slot_of == k % (slots // 2)
            at = pl.ds(n * height + k * rows, rows)
            for p, ref in enumerate((hi_ref, lo_ref)):
                ref[at, :cols] = mine[p]
                ref[at, cols:] = jnp.where(keep, side[p], jnp.zeros_like(side[p]))

    def along_lon(n, many):
        at = pl.ds(n * height, many * height)
        big = dot(hi_ref[at, :], lon_ref[...])
        small = dot(lo_ref[at, :], lon_ref[:, :cols])
        hi, lo = split(big[:, :cols] + big[:, cols:] + small)
        for k in range(many * slots):
            to = pl.ds((n * slots + k) * cols, cols)
            rest = slice(k * rows, (k + 1) * rows)
            mid_ref[:rows, to] = hi[rest]
            mid_ref[rows : 2 * rows, to] = hi[rest]
            mid_ref[2 * rows :, to] = lo[rest]

    def along_lat(n):
        first, h, where = place(n)
        spread = dot(lat_ref[...], mid_ref[:, pl.ds(n * slots * cols, slots * cols)])
        for r, (weights, out) in enumerate(((a_refs, out_a_ref), (own_refs, out_ref), (b_refs, out_b_ref))):
            sums = {}
            for k, (c, m) in enumerate(where):
                piece = spread[r * rows : (r + 1) * rows, k * cols : (k + 1) * cols]
                term = piece * member(weights, m, first + c)
                sums[c] = sums[c] + term if c in sums else term
            for c, total in sums.items():
                at = first - start + c
                out[at] = total if h == 0 else out[at] + total

    units = [range(n, min(n + unit, groups)) for n in range(0, groups, unit)]
    for n in range(len(units) + 2):
        if n < len(units):
            for g in units[n]:
                weigh(g)
        if 0 <= n - 1 < len(units):
            along_lon(units[n - 1][0], len(units[n - 1]))
        if 0 <= n - 2:
            for g in units[n - 2]:
                along_lat(g)


def whole(n):
    return [pl.BlockSpec(memory_space=pltpu.VMEM)] * n


def smooth_call(strip, slots, members, rows, cols, parts, start, size, unit=UNIT):
    block = jax.ShapeDtypeStruct((size, rows, cols), F32)
    planes = size * members
    return pl.pallas_call(
        functools.partial(smooth_kernel, strip, slots, start, unit, parts),
        out_shape=(block,) * 3, in_specs=whole(3 * parts + 7), out_specs=whole(3), name="smooth",
        scratch_shapes=[
            pltpu.VMEM((planes * rows, cols + LANES), BF16),
            pltpu.VMEM((planes * rows, cols + LANES), BF16),
            pltpu.VMEM((3 * rows, planes * cols), BF16),
        ],
        compiler_params=pltpu.CompilerParams(vmem_limit_bytes=GRANT),
    )


def partners(count, first, closed):
    pairs = [(i, (i + 1) % count) for i in range(first, count if closed else count - 1, 2)]
    return sorted(set(pairs + [(j, i) for i, j in pairs]))


def local(grad_tokens, token_index, members, lat_taps, lon_taps):
    ens, lat_count, lon_count = (lax.axis_size(a) for a in ("ens", "lat", "lon"))
    ens_pos, lat_pos, lon_pos = (lax.axis_index(a) for a in ("ens", "lat", "lon"))
    channels, cells = grad_tokens.shape
    rows, cols = token_index.shape
    own_channels = channels // ens
    blocks = lat_count * lon_count
    piece = cells // blocks
    strip = lon_taps.shape[0] - 1
    slots = LANES // strip
    assert cols == LANES and lon_count % 2 == 0 and lat_taps.shape[0] - 1 <= rows

    tokens = lax.dynamic_slice_in_dim(grad_tokens, ens_pos * own_channels, own_channels, 0)
    tokens = tokens.reshape(own_channels, blocks, piece).transpose(1, 0, 2)
    moved = lax.all_to_all(tokens, ("lat", "lon"), split_axis=0, concat_axis=0, tiled=True)
    if piece != LANES:
        moved = moved.transpose(1, 0, 2).reshape(own_channels, cells // LANES, LANES).transpose(1, 0, 2)
    block_id = lat_pos * lon_count + lon_pos
    offset = (token_index // cells) * piece + token_index % cells - block_id * piece

    lat_a, lat_b = partners(lat_count, 0, False), partners(lat_count, 1, False)
    lon_a, lon_b = partners(lon_count, 0, True), partners(lon_count, 1, True)
    if ens == 2:
        given = lax.dynamic_slice_in_dim(members, (1 - ens_pos) * own_channels, own_channels, 1)
        kept = lax.dynamic_slice_in_dim(members, ens_pos * own_channels, own_channels, 1)
        taken = lax.ppermute(given, "ens", [(0, 1), (1, 0)])
        w = [kept, taken]
    else:
        w = [lax.all_to_all(members, "ens", split_axis=1, concat_axis=0, tiled=True)]
    w_a, w_b = [], []
    for block in w:
        w_a.append(lax.ppermute(block, "lat", lat_a))
        w_b.append(lax.ppermute(block, "lat", lat_b))
    count = len(w) * w[0].shape[0]
    per = max(1, slots // count)

    strips = jax.ShapeDtypeStruct((max(1, count // slots), own_channels // per, rows, LANES), BF16)
    smem = pl.BlockSpec(memory_space=pltpu.SMEM)
    strip_a, strip_b, lon_both, lat = pl.pallas_call(
        functools.partial(prepare_kernel, strip, slots, lat_count, len(w)),
        out_shape=(
            strips,
            strips,
            jax.ShapeDtypeStruct((2 * LANES, 2 * cols), BF16),
            jax.ShapeDtypeStruct((3 * rows, 3 * rows), BF16),
        ),
        in_specs=whole(len(w)) + [smem] * 2, out_specs=whole(4), name="prepare",
        compiler_params=pltpu.CompilerParams(vmem_limit_bytes=GRANT),
    )(*w, lat_taps, lon_taps)
    strip_a = lax.ppermute(strip_a, "lon", lon_a)
    strip_b = lax.ppermute(strip_b, "lon", lon_b)

    padded = -(-own_channels // slots) * slots
    edges = jax.ShapeDtypeStruct((padded // slots, rows, LANES), BF16)
    grid, grid_a, grid_b = pl.pallas_call(
        functools.partial(gather_kernel, strip, slots),
        out_shape=(jax.ShapeDtypeStruct((own_channels, rows, cols), BF16), edges, edges),
        in_specs=whole(2), out_specs=whole(3),
        scratch_shapes=[pltpu.VMEM((padded, rows, cols), F32)], name="gather",
        compiler_params=pltpu.CompilerParams(vmem_limit_bytes=GRANT),
    )(moved, offset)
    grid_a = lax.ppermute(grid_a, "lon", lon_a)
    grid_b = lax.ppermute(grid_b, "lon", lon_b)

    out_a, out, out_b = smooth_call(strip, slots, count, rows, cols, len(w), 0, own_channels)(
        *w, *w_a, *w_b, strip_a, strip_b, grid, grid_a, grid_b, lon_both, lat
    )
    out = out + lax.ppermute(out_a, "lat", lat_a) + lax.ppermute(out_b, "lat", lat_b)
    return out / (count - 1)


def solution(mesh):
    in_specs = (P(None, ("lat", "lon")), P("lat", "lon"), P("ens", None, "lat", "lon"), P(), P())
    out_specs = P("ens", "lat", "lon")

    return jax.shard_map(local, mesh=mesh, in_specs=in_specs, out_specs=out_specs, check_vma=False)
```

```python
import functools

import jax
import jax.numpy as jnp
from jax import lax
from jax.experimental import pallas as pl
from jax.experimental.pallas import tpu as pltpu
from jax.sharding import PartitionSpec as P


LANES = 128
F32 = jnp.float32
BF16 = jnp.bfloat16
UNIT = 7
STEPS = 32760.0
GRANT = 24 << 20


def whole(n):
    return [pl.BlockSpec(memory_space=pltpu.VMEM)] * n


def dot(a, b):
    return lax.dot_general(a, b, (((1,), (0,)), ((), ())), preferred_element_type=F32)


def split(v):
    hi = v.astype(BF16)
    return hi, (v - hi.astype(F32)).astype(BF16)


def band(taps, offset):
    total = jnp.zeros(offset.shape, F32)
    for k, tap in enumerate(taps):
        total = jnp.where(offset == k, tap, total)
    return total


def fill_matrices(strip, lat_count, rows, lat_taps_ref, lon_taps_ref, matrix_ref):
    cols = matrix_ref.shape[1] // 2
    count = lon_taps_ref.shape[0]
    iota = lax.broadcasted_iota
    taps = [lon_taps_ref[k] for k in range(count)]
    half = [sum(taps[a] * taps[a - d] for a in range(d, count)) for d in range(count)]
    both = half[:0:-1] + half
    place = iota(jnp.int32, (2 * LANES, cols), 0)
    inner = place % strip
    even = lax.rem(lax.axis_index("lon"), 2) == 0
    after = (place < cols + LANES // 2) == even
    source = jnp.where(place < cols, place, jnp.where(after, cols + inner, inner - strip))
    hi, lo = split(band(both, source - iota(jnp.int32, (2 * LANES, cols), 1) + count - 1))
    matrix_ref[: 2 * LANES, :] = jnp.concatenate([hi, lo], axis=1)
    count = lat_taps_ref.shape[0]
    radius = (count - 1) // 2
    taps = [lat_taps_ref[k] for k in range(count)]
    middle = rows + 2 * radius
    toward = jnp.where(lax.rem(lax.axis_index("lat"), 2) == 0, rows, -rows)
    place = iota(jnp.int32, (3 * rows, middle), 0)
    out_row = place % rows + (1 - place // rows) * toward
    mid_row = iota(jnp.int32, (3 * rows, middle), 1) - radius
    spread = band(taps, mid_row - out_row + radius)
    mid_row = iota(jnp.int32, (middle, rows), 0) - radius
    gather = band(taps[::-1], iota(jnp.int32, (middle, rows), 1) - mid_row + radius)
    whole_row = lax.axis_index("lat") * rows + mid_row
    gather = jnp.where((whole_row >= 0) & (whole_row < lat_count * rows), gather, 0.0)
    hi, lo = split(jnp.dot(spread, gather, precision=lax.Precision.HIGHEST, preferred_element_type=F32))
    matrix_ref[2 * LANES :, : 3 * rows] = jnp.concatenate([hi, lo, hi], axis=1)


def pick_matrix(slot, strip, cols):
    even = lax.rem(lax.axis_index("lon"), 2) == 0
    last = cols - strip
    lane = lax.broadcasted_iota(jnp.int32, (cols, 2 * LANES), 1)
    row = lax.broadcasted_iota(jnp.int32, (cols, 2 * LANES), 0)
    first = jnp.where((lane < LANES) == even, last, 0)
    chosen = (lane % LANES // strip == slot) & (row == first + lane % strip)
    return jnp.where(chosen, 1.0, 0.0).astype(BF16)


def prepare_kernel(strip, slots, lat_count, parts, *refs):
    w_refs, (lat_taps_ref, lon_taps_ref, a_ref, b_ref, matrix_ref) = refs[:parts], refs[parts:]
    each, channels, rows, cols = w_refs[0].shape
    fill_matrices(strip, lat_count, rows, lat_taps_ref, lon_taps_ref, matrix_ref)
    members = each * parts
    per = max(1, slots // members)
    for h in range(max(1, members // slots)):
        total = None
        for k in range(slots):
            c2, m = (k // members, k % members) if members <= slots else (0, h * slots + k)
            plane = w_refs[m // each][m % each].reshape(channels // per, per, rows, cols)[:, c2]
            part = dot(plane.reshape(-1, cols), pick_matrix(k, strip, cols))
            total = part if total is None else total + part
        total = total.astype(BF16)
        a_ref[h] = total[:, :LANES].reshape(channels // per, rows, LANES)
        b_ref[h] = total[:, LANES:].reshape(channels // per, rows, LANES)


def gather_kernel(strip, slots, lon_count, piece, moved_ref, index_ref, grid_ref, a_ref, b_ref, scratch):
    pieces, channels, width = moved_ref.shape
    rows, cols = index_ref.shape
    cells = rows * cols
    block = lax.axis_index("lat") * lon_count + lax.axis_index("lon")
    index = index_ref[...]
    offset = lax.div(index, cells) * piece + lax.rem(index, cells) - block * piece
    scratch[channels:] = jnp.zeros((scratch.shape[0] - channels, rows, cols), F32)
    tokens = jnp.concatenate([moved_ref[n] for n in range(pieces)], axis=1)
    token = lax.broadcasted_iota(jnp.int32, (pieces * width, 2 * cols), 0)
    for i in range(0, rows, 2):
        wanted = jnp.concatenate([offset[i : i + 1], offset[i + 1 : i + 2]], axis=1)
        chosen = jnp.where(token == wanted, 1.0, 0.0).astype(BF16)
        found = dot(tokens, chosen)
        scratch[:channels, i, :] = found[:, :cols]
        scratch[:channels, i + 1, :] = found[:, cols:]
    grid = scratch[...].astype(BF16)
    grid_ref[...] = grid[:channels]
    groups = scratch.shape[0] // slots
    planes = grid.reshape(groups, slots, rows, cols)
    total = None
    for k in range(slots):
        part = dot(planes[:, k].reshape(-1, cols), pick_matrix(k, strip, cols))
        total = part if total is None else total + part
    total = total.astype(BF16)
    a_ref[...] = total[:, :LANES].reshape(groups, rows, LANES)
    b_ref[...] = total[:, LANES:].reshape(groups, rows, LANES)


class Planes:
    def __init__(self, slots, members, channels):
        self.slots, self.members = slots, members
        self.per, self.folds = max(1, slots // members), max(1, members // slots)
        self.groups = channels // self.per * self.folds

    def place(self, n):
        first, h = n // self.folds * self.per, n % self.folds
        if self.folds == 1:
            return first, h, [(k // self.members, k % self.members) for k in range(self.slots)]
        return first, h, [(0, h * self.slots + k) for k in range(self.slots)]

    def stages(self, unit, *steps):
        units = [range(n, min(n + unit, self.groups)) for n in range(0, self.groups, unit)]
        for n in range(len(units) + len(steps) - 1):
            for behind, step in enumerate(steps):
                if 0 <= n - behind < len(units):
                    step(units[n - behind])


def member(refs, m, c):
    each = refs[0].shape[0]
    return refs[m // each][m % each, c].astype(F32)


def inner_kernel(slots, unit, parts, *refs):
    own_refs, (grid_ref, matrix_ref, part_ref, hi_ref, lo_ref) = refs[:parts], refs[parts:]
    each, channels, rows, cols = own_refs[0].shape
    planes = Planes(slots, each * parts, channels)
    height = slots * rows

    def weigh(unit):
        for n in unit:
            first, _, where = planes.place(n)
            for k, (c, m) in enumerate(where):
                at = pl.ds(n * height + k * rows, rows)
                product = member(own_refs, m, first + c) * grid_ref[first + c].astype(F32)
                hi_ref[at, :], lo_ref[at, :] = split(product)

    def along_lon(unit):
        at = pl.ds(unit[0] * height, len(unit) * height)
        big = dot(hi_ref[at, :], matrix_ref[:cols, :])
        small = dot(lo_ref[at, :], matrix_ref[:cols, :cols])
        part_ref[at, :] = big[:, :cols] + big[:, cols:] + small

    planes.stages(unit, weigh, along_lon)


def smooth_kernel(strip, slots, unit, parts, *refs):
    own_refs, a_refs, b_refs = (refs[n * parts : (n + 1) * parts] for n in range(3))
    (strip_a_ref, strip_b_ref, grid_a_ref, grid_b_ref, matrix_ref, part_ref) = refs[3 * parts : 3 * parts + 6]
    out_a_ref, out_ref, out_b_ref, hi_ref, lo_ref, mid_ref, sum_ref, scale_ref = refs[3 * parts + 6 :]
    each, channels, rows, cols = own_refs[0].shape
    members = each * parts
    planes = Planes(slots, members, channels)
    per, folds = planes.per, planes.folds
    half = LANES // 2
    height = slots * rows
    src = lax.broadcasted_iota(jnp.int32, (LANES, LANES), 0)
    dst = lax.broadcasted_iota(jnp.int32, (LANES, LANES), 1)
    dst_channel = dst // strip // members if folds == 1 else jnp.zeros_like(dst)
    lane = lax.broadcasted_iota(jnp.int32, (rows, LANES), 1)
    low = lane < half
    slot_of = (lane % half) // strip
    scale_ref[...] = jnp.zeros_like(scale_ref)

    def weigh(unit):
        for n in unit:
            first, h, _ = planes.place(n)
            expand = src == ((first + dst_channel) % slots) * strip + dst % strip
            expand = jnp.where(expand, 1.0, 0.0).astype(BF16)
            edge_a = strip_a_ref[h, first // per].astype(F32) * dot(grid_a_ref[first // slots], expand)
            edge_b = strip_b_ref[h, first // per].astype(F32) * dot(grid_b_ref[first // slots], expand)
            sides = (
                split(jnp.where(low, edge_a, pltpu.roll(edge_b, half, 1))),
                split(jnp.where(low, pltpu.roll(edge_a, half, 1), edge_b)),
            )
            for k in range(slots):
                side = sides[k * 2 // slots]
                keep = slot_of == k % (slots // 2)
                at = pl.ds(n * height + k * rows, rows)
                for p, ref in enumerate((hi_ref, lo_ref)):
                    ref[at, :] = jnp.where(keep, side[p], jnp.zeros_like(side[p]))

    def along_lon(unit):
        n, many = unit[0], len(unit)
        at = pl.ds(n * height, many * height)
        edge = pl.ds(cols, LANES)
        big = dot(hi_ref[at, :], matrix_ref[edge, :])
        small = dot(lo_ref[at, :], matrix_ref[edge, :cols])
        hi, lo = split(part_ref[at, :] + big[:, :cols] + big[:, cols:] + small)
        for k in range(many * slots):
            to = pl.ds((n * slots + k) * cols, cols)
            rest = slice(k * rows, (k + 1) * rows)
            mid_ref[:rows, to] = hi[rest]
            mid_ref[rows : 2 * rows, to] = hi[rest]
            mid_ref[2 * rows :, to] = lo[rest]

    def send(side, ref, c, total):
        level = code_of(jnp.max(jnp.abs(total), axis=0, keepdims=True))
        scale_ref[side, c : c + 1, :] = level
        ref[c] = to_int16(jnp.floor(total * (STEPS * scale_of(-level)) + 0.5))

    def along_lat(unit):
        for n in unit:
            first, h, where = planes.place(n)
            spread = dot(matrix_ref[cols + LANES :, : 3 * rows], mid_ref[:, pl.ds(n * slots * cols, slots * cols)])
            for r, weights in enumerate((a_refs, own_refs, b_refs)):
                sums = {}
                for k, (c, m) in enumerate(where):
                    piece = spread[r * rows : (r + 1) * rows, k * cols : (k + 1) * cols]
                    term = piece * member(weights, m, first + c)
                    sums[c] = sums[c] + term if c in sums else term
                for c, total in sums.items():
                    at = first + c
                    if h:
                        total = total + sum_ref[r, at]
                    if h < folds - 1:
                        sum_ref[r, at] = total
                    elif r == 1:
                        out_ref[at] = total
                    else:
                        send(r // 2, (out_a_ref, out_b_ref)[r // 2], at, total)

    planes.stages(unit, weigh, along_lon, along_lat)
    for side, ref in enumerate((out_a_ref, out_b_ref)):
        for n in range(channels, ref.shape[0]):
            at = pl.ds((n - channels) * rows, rows)
            ref[n] = to_int16(scale_ref[side, at, :])


def code_of(largest):
    return jnp.ceil(jnp.log2(jnp.maximum(largest, 1e-36)) * 64.0)


def scale_of(level):
    return jnp.exp2(level * (1.0 / 64.0))


def to_int16(v):
    return v.astype(jnp.int32).astype(jnp.int16)


def add_kernel(total, out_ref, a_ref, b_ref, sum_ref, scale_ref):
    channels, rows, _ = out_ref.shape
    for side, ref in enumerate((a_ref, b_ref)):
        for n in range(channels, ref.shape[0]):
            at = pl.ds((n - channels) * rows, rows)
            scale_ref[side, at, :] = scale_of(ref[n].astype(F32)) * (1.0 / STEPS)
    for c in range(channels):
        added = out_ref[c]
        for side, ref in enumerate((a_ref, b_ref)):
            added = added + ref[c].astype(F32) * scale_ref[side, c : c + 1, :]
        sum_ref[c] = added / total


def call(kernel, out_shape, scratch_shapes=(), smem=0):
    def run(*args):
        n = len(args) - smem
        return pl.pallas_call(
            kernel,
            out_shape=out_shape,
            in_specs=whole(n) + [pl.BlockSpec(memory_space=pltpu.SMEM)] * smem,
            out_specs=whole(len(out_shape)) if isinstance(out_shape, tuple) else whole(1)[0],
            scratch_shapes=scratch_shapes,
            compiler_params=pltpu.CompilerParams(vmem_limit_bytes=GRANT),
        )(*args)

    return run


def inner_call(slots, channels, members, rows, cols, parts):
    high = channels * members * rows
    return call(
        functools.partial(inner_kernel, slots, UNIT, parts),
        jax.ShapeDtypeStruct((high, cols), F32),
        [pltpu.VMEM((high, cols), BF16)] * 2,
    )


def smooth_call(strip, slots, channels, members, rows, cols, parts):
    high = channels * members * rows
    extra = -(-channels // rows)
    side = jax.ShapeDtypeStruct((channels + extra, rows, cols), jnp.int16)
    return call(
        functools.partial(smooth_kernel, strip, slots, UNIT, parts),
        (side, jax.ShapeDtypeStruct((channels, rows, cols), F32), side),
        [
            pltpu.VMEM((high, LANES), BF16),
            pltpu.VMEM((high, LANES), BF16),
            pltpu.VMEM((3 * rows, channels * members * cols), BF16),
            pltpu.VMEM((3, channels if members > slots else 1, rows, cols), F32),
            pltpu.VMEM((2, extra * rows, cols), F32),
        ],
    )


def add_call(total, channels, rows, cols):
    return call(
        functools.partial(add_kernel, total),
        jax.ShapeDtypeStruct((channels, rows, cols), F32),
        [pltpu.VMEM((2, -(-channels // rows) * rows, cols), F32)],
    )


def partners(count, first, closed):
    pairs = [(i, (i + 1) % count) for i in range(first, count if closed else count - 1, 2)]
    return sorted(set(pairs + [(j, i) for i, j in pairs]))


def local(grad_tokens, token_index, members, lat_taps, lon_taps):
    ens, lat_count, lon_count = (lax.axis_size(a) for a in ("ens", "lat", "lon"))
    ens_pos = lax.axis_index("ens")
    channels, cells = grad_tokens.shape
    rows, cols = token_index.shape
    own_channels = channels // ens
    blocks = lat_count * lon_count
    piece = cells // blocks
    strip = lon_taps.shape[0] - 1
    slots = LANES // strip
    assert cols == LANES and lon_count % 2 == 0 and lat_taps.shape[0] - 1 <= rows

    tokens = lax.dynamic_slice_in_dim(grad_tokens, ens_pos * own_channels, own_channels, 0)
    tokens = tokens.reshape(own_channels, blocks, piece).transpose(1, 0, 2)
    moved = lax.all_to_all(tokens, ("lat", "lon"), split_axis=0, concat_axis=0, tiled=True)
    if piece != LANES:
        moved = moved.transpose(1, 0, 2).reshape(own_channels, cells // LANES, LANES).transpose(1, 0, 2)

    lat_a, lat_b = partners(lat_count, 0, False), partners(lat_count, 1, False)
    lon_a, lon_b = partners(lon_count, 0, True), partners(lon_count, 1, True)
    if ens == 2:
        given = lax.dynamic_slice_in_dim(members, (1 - ens_pos) * own_channels, own_channels, 1)
        kept = lax.dynamic_slice_in_dim(members, ens_pos * own_channels, own_channels, 1)
        taken = lax.ppermute(given, "ens", [(0, 1), (1, 0)])
        w = [kept, taken]
    else:
        w = [lax.all_to_all(members, "ens", split_axis=1, concat_axis=0, tiled=True)]
    w_a, w_b = [], []
    for block in w:
        w_a.append(lax.ppermute(block, "lat", lat_a))
        w_b.append(lax.ppermute(block, "lat", lat_b))
    count = len(w) * w[0].shape[0]
    per = max(1, slots // count)

    strips = jax.ShapeDtypeStruct((max(1, count // slots), own_channels // per, rows, LANES), BF16)
    smem = pl.BlockSpec(memory_space=pltpu.SMEM)
    strip_a, strip_b, matrix = pl.pallas_call(
        functools.partial(prepare_kernel, strip, slots, lat_count, len(w)),
        out_shape=(
            strips,
            strips,
            jax.ShapeDtypeStruct((2 * LANES + 3 * rows, 2 * cols), BF16),
        ),
        in_specs=whole(len(w)) + [smem] * 2, out_specs=whole(3), name="prepare",
        compiler_params=pltpu.CompilerParams(vmem_limit_bytes=GRANT),
    )(*w, lat_taps, lon_taps)
    strip_a = lax.ppermute(strip_a, "lon", lon_a)
    strip_b = lax.ppermute(strip_b, "lon", lon_b)

    padded = -(-own_channels // slots) * slots
    edges = jax.ShapeDtypeStruct((padded // slots, rows, LANES), BF16)
    grid, grid_a, grid_b = pl.pallas_call(
        functools.partial(gather_kernel, strip, slots, lon_count, piece),
        out_shape=(jax.ShapeDtypeStruct((own_channels, rows, cols), BF16), edges, edges),
        in_specs=whole(2), out_specs=whole(3),
        scratch_shapes=[pltpu.VMEM((padded, rows, cols), F32)], name="gather",
        compiler_params=pltpu.CompilerParams(vmem_limit_bytes=GRANT),
    )(moved, token_index)
    grid_a = lax.ppermute(grid_a, "lon", lon_a)
    grid_b = lax.ppermute(grid_b, "lon", lon_b)

    sizes = (own_channels, count, rows, cols, len(w))
    part = inner_call(slots, *sizes)(*w, grid, matrix)
    out_a, out, out_b = smooth_call(strip, slots, *sizes)(
        *w, *w_a, *w_b, strip_a, strip_b, grid_a, grid_b, matrix, part
    )
    out_a = lax.ppermute(out_a, "lat", lat_a)
    out_b = lax.ppermute(out_b, "lat", lat_b)
    return add_call(count - 1, own_channels, rows, cols)(out, out_a, out_b)


def solution(mesh):
    in_specs = (P(None, ("lat", "lon")), P("lat", "lon"), P("ens", None, "lat", "lon"), P(), P())
    out_specs = P("ens", "lat", "lon")

    return jax.shard_map(local, mesh=mesh, in_specs=in_specs, out_specs=out_specs, check_vma=False)
```

```python
import functools

import jax
import jax.numpy as jnp
from jax import lax
from jax.experimental import pallas as pl
from jax.experimental.pallas import tpu as pltpu
from jax.sharding import PartitionSpec as P


LANES = 128
F32 = jnp.float32
BF16 = jnp.bfloat16
UNIT = 7
STEPS = 32760.0
GRANT = 8 << 20


def whole(n):
    return [pl.BlockSpec(memory_space=pltpu.VMEM)] * n


def dot(a, b):
    return lax.dot_general(a, b, (((1,), (0,)), ((), ())), preferred_element_type=F32)


def split(v):
    hi = v.astype(BF16)
    return hi, (v - hi.astype(F32)).astype(BF16)


def band(taps, offset):
    total = jnp.zeros(offset.shape, F32)
    for k, tap in enumerate(taps):
        total = jnp.where(offset == k, tap, total)
    return total


def fill_matrices(strip, lat_count, rows, lat_taps_ref, lon_taps_ref, matrix_ref):
    cols = matrix_ref.shape[1]
    count = lon_taps_ref.shape[0]
    iota = lax.broadcasted_iota
    taps = [lon_taps_ref[k] for k in range(count)]
    half = [sum(taps[a] * taps[a - d] for a in range(d, count)) for d in range(count)]
    both = half[:0:-1] + half
    place = iota(jnp.int32, (2 * LANES, cols), 0)
    inner = place % strip
    even = lax.rem(lax.axis_index("lon"), 2) == 0
    after = (place < cols + LANES // 2) == even
    source = jnp.where(place < cols, place, jnp.where(after, cols + inner, inner - strip))
    hi, lo = split(band(both, source - iota(jnp.int32, (2 * LANES, cols), 1) + count - 1))
    for n, side in enumerate((slice(0, cols), slice(cols, None))):
        stacked = jnp.concatenate([hi[side], lo[side], hi[side]], axis=0)
        matrix_ref[3 * cols * n : 3 * cols * (n + 1), :] = stacked
    count = lat_taps_ref.shape[0]
    radius = (count - 1) // 2
    taps = [lat_taps_ref[k] for k in range(count)]
    middle = rows + 2 * radius
    toward = jnp.where(lax.rem(lax.axis_index("lat"), 2) == 0, rows, -rows)
    place = iota(jnp.int32, (3 * rows, middle), 0)
    out_row = place % rows + (1 - place // rows) * toward
    mid_row = iota(jnp.int32, (3 * rows, middle), 1) - radius
    spread = band(taps, mid_row - out_row + radius)
    mid_row = iota(jnp.int32, (middle, rows), 0) - radius
    gather = band(taps[::-1], iota(jnp.int32, (middle, rows), 1) - mid_row + radius)
    whole_row = lax.axis_index("lat") * rows + mid_row
    gather = jnp.where((whole_row >= 0) & (whole_row < lat_count * rows), gather, 0.0)
    hi, lo = split(jnp.dot(spread, gather, precision=lax.Precision.HIGHEST, preferred_element_type=F32))
    matrix_ref[6 * cols :, : 3 * rows] = jnp.concatenate([hi, lo, hi], axis=1)


def pick_matrix(slot, strip, cols):
    even = lax.rem(lax.axis_index("lon"), 2) == 0
    last = cols - strip
    lane = lax.broadcasted_iota(jnp.int32, (cols, 2 * LANES), 1)
    row = lax.broadcasted_iota(jnp.int32, (cols, 2 * LANES), 0)
    first = jnp.where((lane < LANES) == even, last, 0)
    chosen = (lane % LANES // strip == slot) & (row == first + lane % strip)
    return jnp.where(chosen, 1.0, 0.0).astype(BF16)


def prepare_kernel(strip, slots, lat_count, parts, *refs):
    w_refs, (lat_taps_ref, lon_taps_ref, a_ref, b_ref, matrix_ref) = refs[:parts], refs[parts:]
    each, channels, rows, cols = w_refs[0].shape
    fill_matrices(strip, lat_count, rows, lat_taps_ref, lon_taps_ref, matrix_ref)
    members = each * parts
    per = max(1, slots // members)
    for h in range(max(1, members // slots)):
        total = None
        for k in range(slots):
            c2, m = (k // members, k % members) if members <= slots else (0, h * slots + k)
            plane = w_refs[m // each][m % each].reshape(channels // per, per, rows, cols)[:, c2]
            part = dot(plane.reshape(-1, cols), pick_matrix(k, strip, cols))
            total = part if total is None else total + part
        total = total.astype(BF16)
        a_ref[h] = total[:, :LANES].reshape(channels // per, rows, LANES)
        b_ref[h] = total[:, LANES:].reshape(channels // per, rows, LANES)


def gather_kernel(strip, slots, lon_count, piece, moved_ref, index_ref, grid_ref, a_ref, b_ref, scratch, stack):
    pieces, channels, width = moved_ref.shape
    rows, cols = index_ref.shape
    cells = rows * cols
    block = lax.axis_index("lat") * lon_count + lax.axis_index("lon")
    index = index_ref[...]
    offset = lax.div(index, cells) * piece + lax.rem(index, cells) - block * piece
    scratch[channels:] = jnp.zeros((scratch.shape[0] - channels, rows, cols), F32)
    high = -(-channels // 8) * 8
    for n in range(pieces):
        stack[n * high : n * high + channels, :] = moved_ref[n]
    place = lax.broadcasted_iota(jnp.int32, (width, 2 * cols), 0)
    many = next(n for n in (8, 4, 2, 1) if pieces % n == 0)
    for i in range(0, rows, 2):
        wanted = jnp.concatenate([offset[i : i + 1], offset[i + 1 : i + 2]], axis=1)
        chosen = jnp.where(place == lax.rem(wanted, width), 1.0, 0.0).astype(BF16)
        source = jnp.broadcast_to(lax.div(wanted, width), (high, 2 * cols))
        found = jnp.zeros((high, 2 * cols), F32)
        for n in range(0, pieces, many):
            some = dot(stack[n * high : (n + many) * high, :], chosen)
            for q in range(many):
                found = jnp.where(source == n + q, some[q * high : (q + 1) * high], found)
        scratch[:channels, i, :] = found[:channels, :cols]
        scratch[:channels, i + 1, :] = found[:channels, cols:]
    grid = scratch[...].astype(BF16)
    grid_ref[...] = grid[:channels]
    groups = scratch.shape[0] // slots
    planes = grid.reshape(groups, slots, rows, cols)
    total = None
    for k in range(slots):
        part = dot(planes[:, k].reshape(-1, cols), pick_matrix(k, strip, cols))
        total = part if total is None else total + part
    total = total.astype(BF16)
    a_ref[...] = total[:, :LANES].reshape(groups, rows, LANES)
    b_ref[...] = total[:, LANES:].reshape(groups, rows, LANES)


class Planes:
    def __init__(self, slots, members, channels):
        self.slots, self.members = slots, members
        self.per, self.folds = max(1, slots // members), max(1, members // slots)
        self.groups = channels // self.per * self.folds

    def place(self, n):
        first, h = n // self.folds * self.per, n % self.folds
        if self.folds == 1:
            return first, h, [(k // self.members, k % self.members) for k in range(self.slots)]
        return first, h, [(0, h * self.slots + k) for k in range(self.slots)]

    def stages(self, unit, *steps):
        units = [range(n, min(n + unit, self.groups)) for n in range(0, self.groups, unit)]
        for n in range(len(units) + len(steps) - 1):
            for behind, step in enumerate(steps):
                if 0 <= n - behind < len(units):
                    step(units[n - behind])


def member(refs, m, c):
    each = refs[0].shape[0]
    return refs[m // each][m % each, c].astype(F32)


def inner_kernel(slots, unit, parts, *refs):
    own_refs, (grid_ref, matrix_ref, part_ref, product_ref) = refs[:parts], refs[parts:]
    each, channels, rows, cols = own_refs[0].shape
    planes = Planes(slots, each * parts, channels)
    height = slots * rows

    def weigh(unit):
        for n in unit:
            first, _, where = planes.place(n)
            for k, (c, m) in enumerate(where):
                at = pl.ds(n * height + k * rows, rows)
                product_ref[at, :] = member(own_refs, m, first + c) * grid_ref[first + c].astype(F32)

    def along_lon(unit):
        at = pl.ds(unit[0] * height, len(unit) * height)
        hi, lo = split(product_ref[at, :])
        part_ref[at, :] = dot(jnp.concatenate([hi, hi, lo], axis=1), matrix_ref[: 3 * cols, :])

    planes.stages(unit, weigh, along_lon)


def outer_kernel(
    strip, slots, unit, members, strip_a_ref, strip_b_ref, grid_a_ref, grid_b_ref, matrix_ref, part_ref,
    mid_ref, side_ref,
):
    cols = part_ref.shape[1]
    folds, pairs, rows, _ = strip_a_ref.shape
    planes = Planes(slots, members, pairs * max(1, slots // members))
    per = planes.per
    half = LANES // 2
    height = slots * rows
    src = lax.broadcasted_iota(jnp.int32, (LANES, LANES), 0)
    dst = lax.broadcasted_iota(jnp.int32, (LANES, LANES), 1)
    dst_channel = dst // strip // members if folds == 1 else jnp.zeros_like(dst)
    lane = lax.broadcasted_iota(jnp.int32, (rows, LANES), 1)
    low = lane < half
    slot_of = (lane % half) // strip
    expands = {}

    def weigh(unit):
        for n in unit:
            first, h, _ = planes.place(n)
            if first % slots not in expands:
                expand = src == ((first + dst_channel) % slots) * strip + dst % strip
                expands[first % slots] = jnp.where(expand, 1.0, 0.0).astype(BF16)
            expand = expands[first % slots]
            edge_a = strip_a_ref[h, first // per].astype(F32) * dot(grid_a_ref[first // slots], expand)
            edge_b = strip_b_ref[h, first // per].astype(F32) * dot(grid_b_ref[first // slots], expand)
            side_ref[2 * n] = jnp.where(low, edge_a, pltpu.roll(edge_b, half, 1))
            side_ref[2 * n + 1] = jnp.where(low, pltpu.roll(edge_a, half, 1), edge_b)

    def along_lon(unit):
        at = pl.ds(unit[0] * height, len(unit) * height)
        edges = []
        for n in unit:
            for s in range(2):
                hi, lo = split(side_ref[2 * n + s])
                none = jnp.zeros_like(hi)
                for k in range(slots // 2):
                    keep = slot_of == k
                    one, two = jnp.where(keep, hi, none), jnp.where(keep, lo, none)
                    edges.append(jnp.concatenate([one, one, two], axis=1))
        edges = jnp.concatenate(edges, axis=0)
        mid_ref[at, :] = part_ref[at, :] + dot(edges, matrix_ref[3 * cols : 6 * cols, :])

    planes.stages(unit, weigh, along_lon)


def spread_kernel(slots, unit, parts, *refs):
    own_refs, a_refs, b_refs = (refs[n * parts : (n + 1) * parts] for n in range(3))
    matrix_ref, mid_ref, out_a_ref, out_ref, out_b_ref, sum_ref, scale_ref = refs[3 * parts :]
    each, channels, rows, cols = own_refs[0].shape
    planes = Planes(slots, each * parts, channels)
    per, folds = planes.per, planes.folds
    height = slots * rows
    scale_ref[...] = jnp.zeros_like(scale_ref)

    def along_lat(unit):
        for n in unit:
            first, h, where = planes.place(n)
            hi, lo = split(mid_ref[pl.ds(n * height, height), :])
            stack = []
            for k in range(slots):
                at = slice(k * rows, (k + 1) * rows)
                stack.append(jnp.concatenate([hi[at], hi[at], lo[at]], axis=0))
            spread = dot(matrix_ref[6 * cols :, : 3 * rows], jnp.concatenate(stack, axis=1))
            for r, weights in enumerate((a_refs, own_refs, b_refs)):
                sums = {}
                for k, (c, m) in enumerate(where):
                    piece = spread[r * rows : (r + 1) * rows, k * cols : (k + 1) * cols]
                    term = piece * member(weights, m, first + c)
                    sums[c] = sums[c] + term if c in sums else term
                for c, total in sums.items():
                    at = first + c
                    if h:
                        total = total + sum_ref[r, at]
                    if r == 1 and h == folds - 1:
                        out_ref[at] = total
                        continue
                    sum_ref[r, at] = total
                    if h == folds - 1:
                        scale_ref[r // 2, at : at + 1, :] = jnp.max(jnp.abs(total), axis=0, keepdims=True)

    def send(unit):
        first, last = planes.place(unit[0])[0], planes.place(unit[-1])[0] + per
        for side, ref in enumerate((out_a_ref, out_b_ref)):
            level = code_of(scale_ref[side, first:last, :])
            scale_ref[side, first:last, :] = level
            factor = STEPS * scale_of(-level)
            for c in range(first, last):
                total = sum_ref[2 * side, c] * factor[c - first : c - first + 1]
                ref[c] = to_int16(jnp.floor(total + 0.5))

    planes.stages(unit, along_lat, send)
    for side, ref in enumerate((out_a_ref, out_b_ref)):
        for n in range(channels, ref.shape[0]):
            at = pl.ds((n - channels) * rows, rows)
            ref[n] = to_int16(scale_ref[side, at, :])


def code_of(largest):
    return jnp.ceil(jnp.log2(jnp.maximum(largest, 1e-36)) * 64.0)


def scale_of(level):
    return jnp.exp2(level * (1.0 / 64.0))


def to_int16(v):
    return v.astype(jnp.int32).astype(jnp.int16)


def add_kernel(total, out_ref, a_ref, b_ref, sum_ref, scale_ref):
    channels, rows, _ = out_ref.shape
    for side, ref in enumerate((a_ref, b_ref)):
        for n in range(channels, ref.shape[0]):
            at = pl.ds((n - channels) * rows, rows)
            scale_ref[side, at, :] = scale_of(ref[n].astype(F32)) * (1.0 / STEPS)
    for c in range(channels):
        added = out_ref[c]
        for side, ref in enumerate((a_ref, b_ref)):
            added = added + ref[c].astype(F32) * scale_ref[side, c : c + 1, :]
        sum_ref[c] = added / total


def call(kernel, out_shape, scratch_shapes=(), smem=0):
    def run(*args):
        n = len(args) - smem
        return pl.pallas_call(
            kernel,
            out_shape=out_shape,
            in_specs=whole(n) + [pl.BlockSpec(memory_space=pltpu.SMEM)] * smem,
            out_specs=whole(len(out_shape)) if isinstance(out_shape, tuple) else whole(1)[0],
            scratch_shapes=scratch_shapes,
            compiler_params=pltpu.CompilerParams(vmem_limit_bytes=GRANT),
        )(*args)

    return run


def inner_call(slots, channels, members, rows, cols, parts):
    high = channels * members * rows
    return call(
        functools.partial(inner_kernel, slots, UNIT, parts),
        jax.ShapeDtypeStruct((high, cols), F32),
        [pltpu.VMEM((high, cols), F32)],
    )


def outer_call(strip, slots, channels, members, rows, cols):
    high = channels * members * rows
    return call(
        functools.partial(outer_kernel, strip, slots, UNIT, members),
        jax.ShapeDtypeStruct((high, cols), F32),
        [pltpu.VMEM((2 * channels * members // slots, rows, LANES), F32)],
    )


def spread_call(slots, channels, members, rows, cols, parts):
    extra = -(-channels // rows)
    side = jax.ShapeDtypeStruct((channels + extra, rows, cols), jnp.int16)
    return call(
        functools.partial(spread_kernel, slots, UNIT, parts),
        (side, jax.ShapeDtypeStruct((channels, rows, cols), F32), side),
        [
            pltpu.VMEM((3, channels, rows, cols), F32),
            pltpu.VMEM((2, extra * rows, cols), F32),
        ],
    )


def add_call(total, channels, rows, cols):
    return call(
        functools.partial(add_kernel, total),
        jax.ShapeDtypeStruct((channels, rows, cols), F32),
        [pltpu.VMEM((2, -(-channels // rows) * rows, cols), F32)],
    )


def partners(count, first, closed):
    pairs = [(i, (i + 1) % count) for i in range(first, count if closed else count - 1, 2)]
    return sorted(set(pairs + [(j, i) for i, j in pairs]))


def local(grad_tokens, token_index, members, lat_taps, lon_taps):
    ens, lat_count, lon_count = (lax.axis_size(a) for a in ("ens", "lat", "lon"))
    ens_pos = lax.axis_index("ens")
    channels, cells = grad_tokens.shape
    rows, cols = token_index.shape
    own_channels = channels // ens
    blocks = lat_count * lon_count
    piece = cells // blocks
    strip = lon_taps.shape[0] - 1
    slots = LANES // strip
    assert cols == LANES and lon_count % 2 == 0 and lat_taps.shape[0] - 1 <= rows

    tokens = lax.dynamic_slice_in_dim(grad_tokens, ens_pos * own_channels, own_channels, 0)
    tokens = tokens.reshape(own_channels, blocks, piece).transpose(1, 0, 2)
    moved = lax.all_to_all(tokens, ("lat", "lon"), split_axis=0, concat_axis=0, tiled=True)
    if piece != LANES:
        moved = moved.transpose(1, 0, 2).reshape(own_channels, cells // LANES, LANES).transpose(1, 0, 2)

    lat_a, lat_b = partners(lat_count, 0, False), partners(lat_count, 1, False)
    lon_a, lon_b = partners(lon_count, 0, True), partners(lon_count, 1, True)
    if ens == 2:
        given = lax.dynamic_slice_in_dim(members, (1 - ens_pos) * own_channels, own_channels, 1)
        kept = lax.dynamic_slice_in_dim(members, ens_pos * own_channels, own_channels, 1)
        taken = lax.ppermute(given, "ens", [(0, 1), (1, 0)])
        w = [kept, taken]
    else:
        w = [lax.all_to_all(members, "ens", split_axis=1, concat_axis=0, tiled=True)]
    w_a, w_b = [], []
    for block in w:
        w_b.append(lax.ppermute(block, "lat", lat_b))
        w_a.append(lax.ppermute(block, "lat", lat_a))
    count = len(w) * w[0].shape[0]
    per = max(1, slots // count)

    strips = jax.ShapeDtypeStruct((max(1, count // slots), own_channels // per, rows, LANES), BF16)
    smem = pl.BlockSpec(memory_space=pltpu.SMEM)
    strip_a, strip_b, matrix = pl.pallas_call(
        functools.partial(prepare_kernel, strip, slots, lat_count, len(w)),
        out_shape=(
            strips,
            strips,
            jax.ShapeDtypeStruct((6 * cols + 3 * rows, cols), BF16),
        ),
        in_specs=whole(len(w)) + [smem] * 2, out_specs=whole(3), name="prepare",
        compiler_params=pltpu.CompilerParams(vmem_limit_bytes=GRANT),
    )(*w, lat_taps, lon_taps)
    strip_b = lax.ppermute(strip_b, "lon", lon_b)
    strip_a = lax.ppermute(strip_a, "lon", lon_a)

    padded = -(-own_channels // slots) * slots
    edges = jax.ShapeDtypeStruct((padded // slots, rows, LANES), BF16)
    grid, grid_a, grid_b = pl.pallas_call(
        functools.partial(gather_kernel, strip, slots, lon_count, piece),
        out_shape=(jax.ShapeDtypeStruct((own_channels, rows, cols), BF16), edges, edges),
        in_specs=whole(2), out_specs=whole(3),
        scratch_shapes=[
            pltpu.VMEM((padded, rows, cols), F32),
            pltpu.VMEM((cells // LANES * (-(-own_channels // 8) * 8), LANES), BF16),
        ], name="gather",
        compiler_params=pltpu.CompilerParams(vmem_limit_bytes=GRANT),
    )(moved, token_index)
    grid_b = lax.ppermute(grid_b, "lon", lon_b)
    grid_a = lax.ppermute(grid_a, "lon", lon_a)

    sizes = (own_channels, count, rows, cols, len(w))
    part = inner_call(slots, *sizes)(*w, grid, matrix)
    mid = outer_call(strip, slots, *sizes[:4])(strip_a, strip_b, grid_a, grid_b, matrix, part)
    out_a, out, out_b = spread_call(slots, *sizes)(*w, *w_a, *w_b, matrix, mid)
    out_b = lax.ppermute(out_b, "lat", lat_b)
    out_a = lax.ppermute(out_a, "lat", lat_a)
    return add_call(count - 1, own_channels, rows, cols)(out, out_a, out_b)


def solution(mesh):
    in_specs = (P(None, ("lat", "lon")), P("lat", "lon"), P("ens", None, "lat", "lon"), P(), P())
    out_specs = P("ens", "lat", "lon")

    return jax.shard_map(local, mesh=mesh, in_specs=in_specs, out_specs=out_specs, check_vma=False)
```

```python
import functools

import jax
import jax.numpy as jnp
from jax import lax
from jax.experimental import pallas as pl
from jax.experimental.pallas import tpu as pltpu
from jax.sharding import PartitionSpec as P


LANES = 128
F32 = jnp.float32
BF16 = jnp.bfloat16
UNIT = 7
STEPS = 32760.0
GRANT = 8 << 20


def whole(n):
    return [pl.BlockSpec(memory_space=pltpu.VMEM)] * n


def dot(a, b):
    return lax.dot_general(a, b, (((1,), (0,)), ((), ())), preferred_element_type=F32)


def split(v):
    hi = v.astype(BF16)
    return hi, (v - hi.astype(F32)).astype(BF16)


def band(taps, offset):
    total = jnp.zeros(offset.shape, F32)
    for k, tap in enumerate(taps):
        total = jnp.where(offset == k, tap, total)
    return total


def fill_matrices(strip, lat_count, rows, lat_taps_ref, lon_taps_ref, matrix_ref, edge_ref):
    cols = matrix_ref.shape[1]
    count = lon_taps_ref.shape[0]
    iota = lax.broadcasted_iota
    taps = [lon_taps_ref[k] for k in range(count)]
    half = [sum(taps[a] * taps[a - d] for a in range(d, count)) for d in range(count)]
    both = half[:0:-1] + half
    place = iota(jnp.int32, (2 * LANES, cols), 0)
    inner = place % strip
    even = lax.rem(lax.axis_index("lon"), 2) == 0
    after = (place < cols + LANES // 2) == even
    source = jnp.where(place < cols, place, jnp.where(after, cols + inner, inner - strip))
    hi, lo = split(band(both, source - iota(jnp.int32, (2 * LANES, cols), 1) + count - 1))
    matrix_ref[: 3 * cols, :] = jnp.concatenate([hi[:cols], lo[:cols], hi[:cols]], axis=0)
    slot = iota(jnp.int32, (LANES, cols), 0) % (LANES // 2) // strip
    for k in range(LANES // 2 // strip):
        one, two = (jnp.where(slot == k, v[cols:], jnp.zeros_like(v[cols:])) for v in (hi, lo))
        edge_ref[:, k * cols : (k + 1) * cols] = jnp.concatenate([one, two, one], axis=0)
    count = lat_taps_ref.shape[0]
    radius = (count - 1) // 2
    taps = [lat_taps_ref[k] for k in range(count)]
    middle = rows + 2 * radius
    toward = jnp.where(lax.rem(lax.axis_index("lat"), 2) == 0, rows, -rows)
    place = iota(jnp.int32, (3 * rows, middle), 0)
    out_row = place % rows + (1 - place // rows) * toward
    mid_row = iota(jnp.int32, (3 * rows, middle), 1) - radius
    spread = band(taps, mid_row - out_row + radius)
    mid_row = iota(jnp.int32, (middle, rows), 0) - radius
    gather = band(taps[::-1], iota(jnp.int32, (middle, rows), 1) - mid_row + radius)
    whole_row = lax.axis_index("lat") * rows + mid_row
    gather = jnp.where((whole_row >= 0) & (whole_row < lat_count * rows), gather, 0.0)
    hi, lo = split(jnp.dot(spread, gather, precision=lax.Precision.HIGHEST, preferred_element_type=F32))
    matrix_ref[3 * cols :, : 3 * rows] = jnp.concatenate([hi, lo, hi], axis=1)


def pick_matrix(slot, strip, cols):
    even = lax.rem(lax.axis_index("lon"), 2) == 0
    last = cols - strip
    lane = lax.broadcasted_iota(jnp.int32, (cols, 2 * LANES), 1)
    row = lax.broadcasted_iota(jnp.int32, (cols, 2 * LANES), 0)
    first = jnp.where((lane < LANES) == even, last, 0)
    chosen = (lane % LANES // strip == slot) & (row == first + lane % strip)
    return jnp.where(chosen, 1.0, 0.0).astype(BF16)


def prepare_kernel(strip, slots, lat_count, parts, *refs):
    w_refs, (lat_taps_ref, lon_taps_ref, a_ref, b_ref, matrix_ref, edge_ref) = refs[:parts], refs[parts:]
    each, channels, rows, cols = w_refs[0].shape
    fill_matrices(strip, lat_count, rows, lat_taps_ref, lon_taps_ref, matrix_ref, edge_ref)
    members = each * parts
    per = max(1, slots // members)
    for h in range(max(1, members // slots)):
        total = None
        for k in range(slots):
            c2, m = (k // members, k % members) if members <= slots else (0, h * slots + k)
            plane = w_refs[m // each][m % each].reshape(channels // per, per, rows, cols)[:, c2]
            part = dot(plane.reshape(-1, cols), pick_matrix(k, strip, cols))
            total = part if total is None else total + part
        total = total.astype(BF16)
        a_ref[h] = total[:, :LANES].reshape(channels // per, rows, LANES)
        b_ref[h] = total[:, LANES:].reshape(channels // per, rows, LANES)


def gather_kernel(strip, slots, lon_count, piece, moved_ref, index_ref, grid_ref, a_ref, b_ref, scratch, stack):
    pieces, channels, width = moved_ref.shape
    rows, cols = index_ref.shape
    cells = rows * cols
    block = lax.axis_index("lat") * lon_count + lax.axis_index("lon")
    index = index_ref[...]
    offset = lax.div(index, cells) * piece + lax.rem(index, cells) - block * piece
    scratch[channels:] = jnp.zeros((scratch.shape[0] - channels, rows, cols), F32)
    high = -(-channels // 8) * 8
    for n in range(pieces):
        stack[n * high : n * high + channels, :] = moved_ref[n]
    place = lax.broadcasted_iota(jnp.int32, (width, 2 * cols), 0)
    many = next(n for n in (16, 8, 4, 2, 1) if pieces % n == 0)
    for i in range(0, rows, 2):
        wanted = jnp.concatenate([offset[i : i + 1], offset[i + 1 : i + 2]], axis=1)
        chosen = jnp.where(place == lax.rem(wanted, width), 1.0, 0.0).astype(BF16)
        source = jnp.broadcast_to(lax.div(wanted, width), (high, 2 * cols))
        found = jnp.zeros((high, 2 * cols), F32)
        for n in range(0, pieces, many):
            some = dot(stack[n * high : (n + many) * high, :], chosen)
            for q in range(many):
                found = jnp.where(source == n + q, some[q * high : (q + 1) * high], found)
        scratch[:channels, i, :] = found[:channels, :cols]
        scratch[:channels, i + 1, :] = found[:channels, cols:]
    grid = scratch[...].astype(BF16)
    grid_ref[...] = grid[:channels]
    groups = scratch.shape[0] // slots
    planes = grid.reshape(groups, slots, rows, cols)
    total = None
    for k in range(slots):
        part = dot(planes[:, k].reshape(-1, cols), pick_matrix(k, strip, cols))
        total = part if total is None else total + part
    total = total.astype(BF16)
    a_ref[...] = total[:, :LANES].reshape(groups, rows, LANES)
    b_ref[...] = total[:, LANES:].reshape(groups, rows, LANES)


class Planes:
    def __init__(self, slots, members, channels):
        self.slots, self.members = slots, members
        self.per, self.folds = max(1, slots // members), max(1, members // slots)
        self.groups = channels // self.per * self.folds

    def place(self, n):
        first, h = n // self.folds * self.per, n % self.folds
        if self.folds == 1:
            return first, h, [(k // self.members, k % self.members) for k in range(self.slots)]
        return first, h, [(0, h * self.slots + k) for k in range(self.slots)]

    def stages(self, unit, *steps):
        units = [range(n, min(n + unit, self.groups)) for n in range(0, self.groups, unit)]
        for n in range(len(units) + len(steps) - 1):
            for behind, step in enumerate(steps):
                if 0 <= n - behind < len(units):
                    step(units[n - behind])


def member(refs, m, c):
    each = refs[0].shape[0]
    return refs[m // each][m % each, c].astype(F32)


def inner_kernel(slots, unit, parts, *refs):
    own_refs = refs[:parts]
    grid_ref, matrix_ref, strip_a_ref, strip_b_ref, part_ref, near_a_ref, near_b_ref, product_ref = refs[parts:]
    near_a_ref[...], near_b_ref[...] = strip_a_ref[...], strip_b_ref[...]
    each, channels, rows, cols = own_refs[0].shape
    planes = Planes(slots, each * parts, channels)
    height = slots * rows

    def weigh(unit):
        for n in unit:
            first, _, where = planes.place(n)
            for k, (c, m) in enumerate(where):
                at = pl.ds(n * height + k * rows, rows)
                product_ref[at, :] = member(own_refs, m, first + c) * grid_ref[first + c].astype(F32)

    def along_lon(unit):
        at = pl.ds(unit[0] * height, len(unit) * height)
        hi, lo = split(product_ref[at, :])
        part_ref[at, :] = dot(jnp.concatenate([hi, hi, lo], axis=1), matrix_ref[: 3 * cols, :])

    planes.stages(unit, weigh, along_lon)


def outer_kernel(
    strip, slots, unit, members, strip_a_ref, strip_b_ref, grid_a_ref, grid_b_ref, edge_ref, part_ref,
    mid_ref, side_ref,
):
    cols = part_ref.shape[1]
    folds, pairs, rows, _ = strip_a_ref.shape
    planes = Planes(slots, members, pairs * max(1, slots // members))
    per = planes.per
    half = LANES // 2
    src = lax.broadcasted_iota(jnp.int32, (LANES, LANES), 0)
    dst = lax.broadcasted_iota(jnp.int32, (LANES, LANES), 1)
    dst_channel = dst // strip // members if folds == 1 else jnp.zeros_like(dst)
    lane = lax.broadcasted_iota(jnp.int32, (rows, LANES), 1)
    low = lane < half
    expands = {}

    def weigh(unit):
        for n in unit:
            first, h, _ = planes.place(n)
            if first % slots not in expands:
                expand = src == ((first + dst_channel) % slots) * strip + dst % strip
                expands[first % slots] = jnp.where(expand, 1.0, 0.0).astype(BF16)
            expand = expands[first % slots]
            edge_a = strip_a_ref[h, first // per].astype(F32) * dot(grid_a_ref[first // slots], expand)
            edge_b = strip_b_ref[h, first // per].astype(F32) * dot(grid_b_ref[first // slots], expand)
            side_ref[pl.ds(2 * n * rows, rows), :] = jnp.where(low, edge_a, pltpu.roll(edge_b, half, 1))
            side_ref[pl.ds((2 * n + 1) * rows, rows), :] = jnp.where(low, pltpu.roll(edge_a, half, 1), edge_b)

    def along_lon(unit):
        hi, lo = split(side_ref[pl.ds(2 * unit[0] * rows, 2 * len(unit) * rows), :])
        found = dot(jnp.concatenate([hi, hi, lo], axis=1), edge_ref[...])
        for n in range(2 * len(unit)):
            for k in range(slots // 2):
                at = pl.ds(((2 * unit[0] + n) * (slots // 2) + k) * rows, rows)
                piece = found[n * rows : (n + 1) * rows, k * cols : (k + 1) * cols]
                mid_ref[at, :] = part_ref[at, :] + piece

    planes.stages(unit, weigh, along_lon)


def spread_kernel(slots, unit, parts, *refs):
    own_refs, a_refs, b_refs = (refs[n * parts : (n + 1) * parts] for n in range(3))
    matrix_ref, mid_ref, out_a_ref, out_ref, out_b_ref, sum_ref, scale_ref = refs[3 * parts :]
    each, channels, rows, cols = own_refs[0].shape
    planes = Planes(slots, each * parts, channels)
    per, folds = planes.per, planes.folds
    height = slots * rows
    scale_ref[...] = jnp.zeros_like(scale_ref)

    def along_lat(unit):
        for n in unit:
            first, h, where = planes.place(n)
            hi, lo = split(mid_ref[pl.ds(n * height, height), :])
            stack = []
            for k in range(slots):
                at = slice(k * rows, (k + 1) * rows)
                stack.append(jnp.concatenate([hi[at], hi[at], lo[at]], axis=0))
            spread = dot(matrix_ref[3 * cols :, : 3 * rows], jnp.concatenate(stack, axis=1))
            for r, weights in enumerate((a_refs, own_refs, b_refs)):
                sums = {}
                for k, (c, m) in enumerate(where):
                    piece = spread[r * rows : (r + 1) * rows, k * cols : (k + 1) * cols]
                    term = piece * member(weights, m, first + c)
                    sums[c] = sums[c] + term if c in sums else term
                for c, total in sums.items():
                    at = first + c
                    if h:
                        total = total + sum_ref[r, at]
                    if r == 1 and h == folds - 1:
                        out_ref[at] = total
                        continue
                    sum_ref[r, at] = total
                    if h == folds - 1:
                        scale_ref[r // 2, at : at + 1, :] = jnp.max(jnp.abs(total), axis=0, keepdims=True)

    def send(unit):
        first, last = planes.place(unit[0])[0], planes.place(unit[-1])[0] + per
        for side, ref in enumerate((out_a_ref, out_b_ref)):
            level = code_of(scale_ref[side, first:last, :])
            scale_ref[side, first:last, :] = level
            factor = STEPS * scale_of(-level)
            for c in range(first, last):
                total = sum_ref[2 * side, c] * factor[c - first : c - first + 1]
                ref[c] = to_int16(jnp.floor(total + 0.5))

    planes.stages(unit, along_lat, send)
    for side, ref in enumerate((out_a_ref, out_b_ref)):
        for n in range(channels, ref.shape[0]):
            at = pl.ds((n - channels) * rows, rows)
            ref[n] = to_int16(scale_ref[side, at, :])


def code_of(largest):
    return jnp.ceil(jnp.log2(jnp.maximum(largest, 1e-36)) * 64.0)


def scale_of(level):
    return jnp.exp2(level * (1.0 / 64.0))


def to_int16(v):
    return v.astype(jnp.int32).astype(jnp.int16)


def add_kernel(total, out_ref, a_ref, b_ref, sum_ref, scale_ref):
    channels, rows, _ = out_ref.shape
    for side, ref in enumerate((a_ref, b_ref)):
        for n in range(channels, ref.shape[0]):
            at = pl.ds((n - channels) * rows, rows)
            scale_ref[side, at, :] = scale_of(ref[n].astype(F32)) * (1.0 / STEPS)
    for c in range(channels):
        added = out_ref[c]
        for side, ref in enumerate((a_ref, b_ref)):
            added = added + ref[c].astype(F32) * scale_ref[side, c : c + 1, :]
        sum_ref[c] = added / total


def call(kernel, out_shape, scratch_shapes=(), smem=0):
    def run(*args):
        n = len(args) - smem
        return pl.pallas_call(
            kernel,
            out_shape=out_shape,
            in_specs=whole(n) + [pl.BlockSpec(memory_space=pltpu.SMEM)] * smem,
            out_specs=whole(len(out_shape)) if isinstance(out_shape, tuple) else whole(1)[0],
            scratch_shapes=scratch_shapes,
            compiler_params=pltpu.CompilerParams(vmem_limit_bytes=GRANT),
        )(*args)

    return run


def inner_call(strips, slots, channels, members, rows, cols, parts):
    high = channels * members * rows
    return call(
        functools.partial(inner_kernel, slots, UNIT, parts),
        (jax.ShapeDtypeStruct((high, cols), F32), strips, strips),
        [pltpu.VMEM((high, cols), F32)],
    )


def outer_call(strip, slots, channels, members, rows, cols):
    high = channels * members * rows
    return call(
        functools.partial(outer_kernel, strip, slots, UNIT, members),
        jax.ShapeDtypeStruct((high, cols), F32),
        [pltpu.VMEM((2 * channels * members // slots * rows, LANES), F32)],
    )


def spread_call(slots, channels, members, rows, cols, parts):
    extra = -(-channels // rows)
    side = jax.ShapeDtypeStruct((channels + extra, rows, cols), jnp.int16)
    return call(
        functools.partial(spread_kernel, slots, UNIT, parts),
        (side, jax.ShapeDtypeStruct((channels, rows, cols), F32), side),
        [
            pltpu.VMEM((3, channels, rows, cols), F32),
            pltpu.VMEM((2, extra * rows, cols), F32),
        ],
    )


def add_call(total, channels, rows, cols):
    return call(
        functools.partial(add_kernel, total),
        jax.ShapeDtypeStruct((channels, rows, cols), F32),
        [pltpu.VMEM((2, -(-channels // rows) * rows, cols), F32)],
    )


def partners(count, first, closed):
    pairs = [(i, (i + 1) % count) for i in range(first, count if closed else count - 1, 2)]
    return sorted(set(pairs + [(j, i) for i, j in pairs]))


def local(grad_tokens, token_index, members, lat_taps, lon_taps):
    ens, lat_count, lon_count = (lax.axis_size(a) for a in ("ens", "lat", "lon"))
    ens_pos = lax.axis_index("ens")
    channels, cells = grad_tokens.shape
    rows, cols = token_index.shape
    own_channels = channels // ens
    blocks = lat_count * lon_count
    piece = cells // blocks
    strip = lon_taps.shape[0] - 1
    slots = LANES // strip
    assert cols == LANES and lon_count % 2 == 0 and lat_taps.shape[0] - 1 <= rows

    tokens = lax.dynamic_slice_in_dim(grad_tokens, ens_pos * own_channels, own_channels, 0)
    tokens = tokens.reshape(own_channels, blocks, piece).transpose(1, 0, 2)
    moved = lax.all_to_all(tokens, ("lat", "lon"), split_axis=0, concat_axis=0, tiled=True)
    if piece != LANES:
        moved = moved.transpose(1, 0, 2).reshape(own_channels, cells // LANES, LANES).transpose(1, 0, 2)

    lat_a, lat_b = partners(lat_count, 0, False), partners(lat_count, 1, False)
    lon_a, lon_b = partners(lon_count, 0, True), partners(lon_count, 1, True)
    if ens == 2:
        given = lax.dynamic_slice_in_dim(members, (1 - ens_pos) * own_channels, own_channels, 1)
        kept = lax.dynamic_slice_in_dim(members, ens_pos * own_channels, own_channels, 1)
        taken = lax.ppermute(given, "ens", [(0, 1), (1, 0)])
        w = [kept, taken]
    else:
        w = [lax.all_to_all(members, "ens", split_axis=1, concat_axis=0, tiled=True)]
    w_a, w_b = [], []
    for block in w:
        w_b.append(lax.ppermute(block, "lat", lat_b))
        w_a.append(lax.ppermute(block, "lat", lat_a))
    count = len(w) * w[0].shape[0]
    per = max(1, slots // count)

    strips = jax.ShapeDtypeStruct((max(1, count // slots), own_channels // per, rows, LANES), BF16)
    smem = pl.BlockSpec(memory_space=pltpu.SMEM)
    strip_a, strip_b, matrix, edge_matrix = pl.pallas_call(
        functools.partial(prepare_kernel, strip, slots, lat_count, len(w)),
        out_shape=(
            strips,
            strips,
            jax.ShapeDtypeStruct((3 * cols + 3 * rows, cols), BF16),
            jax.ShapeDtypeStruct((3 * LANES, slots // 2 * cols), BF16),
        ),
        in_specs=whole(len(w)) + [smem] * 2, out_specs=whole(4), name="prepare",
        compiler_params=pltpu.CompilerParams(vmem_limit_bytes=GRANT),
    )(*w, lat_taps, lon_taps)
    strip_b = lax.ppermute(strip_b, "lon", lon_b)
    strip_a = lax.ppermute(strip_a, "lon", lon_a)

    padded = -(-own_channels // slots) * slots
    edges = jax.ShapeDtypeStruct((padded // slots, rows, LANES), BF16)
    grid, grid_a, grid_b = pl.pallas_call(
        functools.partial(gather_kernel, strip, slots, lon_count, piece),
        out_shape=(jax.ShapeDtypeStruct((own_channels, rows, cols), BF16), edges, edges),
        in_specs=whole(2), out_specs=whole(3),
        scratch_shapes=[
            pltpu.VMEM((padded, rows, cols), F32),
            pltpu.VMEM((cells // LANES * (-(-own_channels // 8) * 8), LANES), BF16),
        ], name="gather",
        compiler_params=pltpu.CompilerParams(vmem_limit_bytes=GRANT),
    )(moved, token_index)
    grid_b = lax.ppermute(grid_b, "lon", lon_b)
    grid_a = lax.ppermute(grid_a, "lon", lon_a)

    sizes = (own_channels, count, rows, cols, len(w))
    part, strip_a, strip_b = inner_call(strips, slots, *sizes)(*w, grid, matrix, strip_a, strip_b)
    mid = outer_call(strip, slots, *sizes[:4])(strip_a, strip_b, grid_a, grid_b, edge_matrix, part)
    out_a, out, out_b = spread_call(slots, *sizes)(*w, *w_a, *w_b, matrix, mid)
    out_b = lax.ppermute(out_b, "lat", lat_b)
    out_a = lax.ppermute(out_a, "lat", lat_a)
    return add_call(count - 1, own_channels, rows, cols)(out, out_a, out_b)


def solution(mesh):
    in_specs = (P(None, ("lat", "lon")), P("lat", "lon"), P("ens", None, "lat", "lon"), P(), P())
    out_specs = P("ens", "lat", "lon")

    return jax.shard_map(local, mesh=mesh, in_specs=in_specs, out_specs=out_specs, check_vma=False)
```

```python
import functools

import jax
import jax.numpy as jnp
from jax import lax
from jax.experimental import pallas as pl
from jax.experimental.pallas import tpu as pltpu
from jax.sharding import PartitionSpec as P


LANES = 128
F32 = jnp.float32
BF16 = jnp.bfloat16
UNIT = 7
STEPS = 32760.0
GRANT = 8 << 20


def whole(n):
    return [pl.BlockSpec(memory_space=pltpu.VMEM)] * n


def dot(a, b):
    return lax.dot_general(a, b, (((1,), (0,)), ((), ())), preferred_element_type=F32)


def split(v):
    hi = v.astype(BF16)
    return hi, (v - hi.astype(F32)).astype(BF16)


def band(taps, offset):
    total = jnp.zeros(offset.shape, F32)
    for k, tap in enumerate(taps):
        total = jnp.where(offset == k, tap, total)
    return total


def matrix_kernel(strip, lat_count, rows, lat_taps_ref, lon_taps_ref, matrix_ref, edge_ref):
    cols = matrix_ref.shape[1]
    count = lon_taps_ref.shape[0]
    iota = lax.broadcasted_iota
    taps = [lon_taps_ref[k] for k in range(count)]
    half = [sum(taps[a] * taps[a - d] for a in range(d, count)) for d in range(count)]
    both = half[:0:-1] + half
    place = iota(jnp.int32, (2 * LANES, cols), 0)
    inner = place % strip
    even = lax.rem(lax.axis_index("lon"), 2) == 0
    after = (place < cols + LANES // 2) == even
    source = jnp.where(place < cols, place, jnp.where(after, cols + inner, inner - strip))
    hi, lo = split(band(both, source - iota(jnp.int32, (2 * LANES, cols), 1) + count - 1))
    matrix_ref[: 3 * cols, :] = jnp.concatenate([hi[:cols], lo[:cols], hi[:cols]], axis=0)
    slot = iota(jnp.int32, (LANES, cols), 0) % (LANES // 2) // strip
    for k in range(LANES // 2 // strip):
        one, two = (jnp.where(slot == k, v[cols:], jnp.zeros_like(v[cols:])) for v in (hi, lo))
        edge_ref[:, k * cols : (k + 1) * cols] = jnp.concatenate([one, two, one], axis=0)
    count = lat_taps_ref.shape[0]
    radius = (count - 1) // 2
    taps = [lat_taps_ref[k] for k in range(count)]
    middle = rows + 2 * radius
    toward = jnp.where(lax.rem(lax.axis_index("lat"), 2) == 0, rows, -rows)
    place = iota(jnp.int32, (3 * rows, middle), 0)
    out_row = place % rows + (1 - place // rows) * toward
    mid_row = iota(jnp.int32, (3 * rows, middle), 1) - radius
    spread = band(taps, mid_row - out_row + radius)
    mid_row = iota(jnp.int32, (middle, rows), 0) - radius
    gather = band(taps[::-1], iota(jnp.int32, (middle, rows), 1) - mid_row + radius)
    whole_row = lax.axis_index("lat") * rows + mid_row
    gather = jnp.where((whole_row >= 0) & (whole_row < lat_count * rows), gather, 0.0)
    hi, lo = split(jnp.dot(spread, gather, precision=lax.Precision.HIGHEST, preferred_element_type=F32))
    matrix_ref[3 * cols :, : 3 * rows] = jnp.concatenate([hi, lo, hi], axis=1)


def pick_matrix(slot, strip, cols):
    even = lax.rem(lax.axis_index("lon"), 2) == 0
    last = cols - strip
    lane = lax.broadcasted_iota(jnp.int32, (cols, 2 * LANES), 1)
    row = lax.broadcasted_iota(jnp.int32, (cols, 2 * LANES), 0)
    first = jnp.where((lane < LANES) == even, last, 0)
    chosen = (lane % LANES // strip == slot) & (row == first + lane % strip)
    return jnp.where(chosen, 1.0, 0.0).astype(BF16)


def pack_kernel(strip, slots, parts, lon_count, piece, *refs):
    w_refs, (index_ref, a_ref, b_ref, offset_ref, landed, sem) = refs[:parts], refs[parts:]
    copy = pltpu.make_async_copy(index_ref, landed, sem)
    copy.start()
    each, channels, rows, cols = w_refs[0].shape
    members = each * parts
    per = max(1, slots // members)
    for h in range(max(1, members // slots)):
        total = None
        for k in range(slots):
            c2, m = (k // members, k % members) if members <= slots else (0, h * slots + k)
            plane = w_refs[m // each][m % each].reshape(channels // per, per, rows, cols)[:, c2]
            part = dot(plane.reshape(-1, cols), pick_matrix(k, strip, cols))
            total = part if total is None else total + part
        total = total.astype(BF16)
        a_ref[h] = total[:, :LANES].reshape(channels // per, rows, LANES)
        b_ref[h] = total[:, LANES:].reshape(channels // per, rows, LANES)
    copy.wait()
    cells = rows * cols
    block = lax.axis_index("lat") * lon_count + lax.axis_index("lon")
    index = landed[...]
    offset_ref[...] = lax.div(index, cells) * piece + lax.rem(index, cells) - block * piece


def gather_kernel(strip, slots, moved_ref, offset_ref, grid_ref, a_ref, b_ref, scratch, stack):
    pieces, channels, width = moved_ref.shape
    rows, cols = offset_ref.shape
    offset = offset_ref[...]
    scratch[channels:] = jnp.zeros((scratch.shape[0] - channels, rows, cols), F32)
    high = -(-channels // 8) * 8
    for n in range(pieces):
        stack[n * high : n * high + channels, :] = moved_ref[n]
    place = lax.broadcasted_iota(jnp.int32, (width, 2 * cols), 0)
    many = next(n for n in (16, 8, 4, 2, 1) if pieces % n == 0)
    for i in range(0, rows, 2):
        wanted = jnp.concatenate([offset[i : i + 1], offset[i + 1 : i + 2]], axis=1)
        chosen = jnp.where(place == lax.rem(wanted, width), 1.0, 0.0).astype(BF16)
        source = jnp.broadcast_to(lax.div(wanted, width), (high, 2 * cols))
        found = jnp.zeros((high, 2 * cols), F32)
        for n in range(0, pieces, many):
            some = dot(stack[n * high : (n + many) * high, :], chosen)
            for q in range(many):
                found = jnp.where(source == n + q, some[q * high : (q + 1) * high], found)
        scratch[:channels, i, :] = found[:channels, :cols]
        scratch[:channels, i + 1, :] = found[:channels, cols:]
    grid = scratch[...].astype(BF16)
    grid_ref[...] = grid[:channels]
    groups = scratch.shape[0] // slots
    planes = grid.reshape(groups, slots, rows, cols)
    total = None
    for k in range(slots):
        part = dot(planes[:, k].reshape(-1, cols), pick_matrix(k, strip, cols))
        total = part if total is None else total + part
    total = total.astype(BF16)
    a_ref[...] = total[:, :LANES].reshape(groups, rows, LANES)
    b_ref[...] = total[:, LANES:].reshape(groups, rows, LANES)


class Planes:
    def __init__(self, slots, members, channels):
        self.slots, self.members = slots, members
        self.per, self.folds = max(1, slots // members), max(1, members // slots)
        self.groups = channels // self.per * self.folds

    def place(self, n):
        first, h = n // self.folds * self.per, n % self.folds
        if self.folds == 1:
            return first, h, [(k // self.members, k % self.members) for k in range(self.slots)]
        return first, h, [(0, h * self.slots + k) for k in range(self.slots)]

    def stages(self, unit, *steps):
        units = [range(n, min(n + unit, self.groups)) for n in range(0, self.groups, unit)]
        for n in range(len(units) + len(steps) - 1):
            for behind, step in enumerate(steps):
                if 0 <= n - behind < len(units):
                    step(units[n - behind])


def member(refs, m, c):
    each = refs[0].shape[0]
    return refs[m // each][m % each, c].astype(F32)


def inner_kernel(slots, unit, parts, *refs):
    own_refs = refs[:parts]
    grid_ref, matrix_ref, strip_a_ref, strip_b_ref, part_ref, near_a_ref, near_b_ref, product_ref = refs[parts:]
    near_a_ref[...], near_b_ref[...] = strip_a_ref[...], strip_b_ref[...]
    each, channels, rows, cols = own_refs[0].shape
    planes = Planes(slots, each * parts, channels)
    height = slots * rows

    def weigh(unit):
        for n in unit:
            first, _, where = planes.place(n)
            for k, (c, m) in enumerate(where):
                at = pl.ds(n * height + k * rows, rows)
                product_ref[at, :] = member(own_refs, m, first + c) * grid_ref[first + c].astype(F32)

    def along_lon(unit):
        at = pl.ds(unit[0] * height, len(unit) * height)
        hi, lo = split(product_ref[at, :])
        part_ref[at, :] = dot(jnp.concatenate([hi, hi, lo], axis=1), matrix_ref[: 3 * cols, :])

    planes.stages(unit, weigh, along_lon)


def outer_kernel(
    strip, slots, unit, members, strip_a_ref, strip_b_ref, grid_a_ref, grid_b_ref, edge_ref, part_ref,
    mid_ref, side_ref,
):
    cols = part_ref.shape[1]
    folds, pairs, rows, _ = strip_a_ref.shape
    planes = Planes(slots, members, pairs * max(1, slots // members))
    per = planes.per
    half = LANES // 2
    src = lax.broadcasted_iota(jnp.int32, (LANES, LANES), 0)
    dst = lax.broadcasted_iota(jnp.int32, (LANES, LANES), 1)
    dst_channel = dst // strip // members if folds == 1 else jnp.zeros_like(dst)
    lane = lax.broadcasted_iota(jnp.int32, (rows, LANES), 1)
    low = lane < half
    expands = {}

    def weigh(unit):
        for n in unit:
            first, h, _ = planes.place(n)
            if first % slots not in expands:
                expand = src == ((first + dst_channel) % slots) * strip + dst % strip
                expands[first % slots] = jnp.where(expand, 1.0, 0.0).astype(BF16)
            expand = expands[first % slots]
            edge_a = strip_a_ref[h, first // per].astype(F32) * dot(grid_a_ref[first // slots], expand)
            edge_b = strip_b_ref[h, first // per].astype(F32) * dot(grid_b_ref[first // slots], expand)
            side_ref[pl.ds(2 * n * rows, rows), :] = jnp.where(low, edge_a, pltpu.roll(edge_b, half, 1))
            side_ref[pl.ds((2 * n + 1) * rows, rows), :] = jnp.where(low, pltpu.roll(edge_a, half, 1), edge_b)

    def along_lon(unit):
        hi, lo = split(side_ref[pl.ds(2 * unit[0] * rows, 2 * len(unit) * rows), :])
        found = dot(jnp.concatenate([hi, hi, lo], axis=1), edge_ref[...])
        for n in range(2 * len(unit)):
            for k in range(slots // 2):
                at = pl.ds(((2 * unit[0] + n) * (slots // 2) + k) * rows, rows)
                piece = found[n * rows : (n + 1) * rows, k * cols : (k + 1) * cols]
                mid_ref[at, :] = part_ref[at, :] + piece

    planes.stages(unit, weigh, along_lon)


def spread_kernel(slots, unit, parts, *refs):
    own_refs, a_refs, b_refs = (refs[n * parts : (n + 1) * parts] for n in range(3))
    matrix_ref, mid_ref, out_a_ref, out_ref, out_b_ref, sum_ref, scale_ref = refs[3 * parts :]
    each, channels, rows, cols = own_refs[0].shape
    planes = Planes(slots, each * parts, channels)
    per, folds = planes.per, planes.folds
    height = slots * rows
    scale_ref[...] = jnp.zeros_like(scale_ref)

    def along_lat(unit):
        for n in unit:
            first, h, where = planes.place(n)
            hi, lo = split(mid_ref[pl.ds(n * height, height), :])
            stack = []
            for k in range(slots):
                at = slice(k * rows, (k + 1) * rows)
                stack.append(jnp.concatenate([hi[at], hi[at], lo[at]], axis=0))
            spread = dot(matrix_ref[3 * cols :, : 3 * rows], jnp.concatenate(stack, axis=1))
            for r, weights in enumerate((a_refs, own_refs, b_refs)):
                sums = {}
                for k, (c, m) in enumerate(where):
                    piece = spread[r * rows : (r + 1) * rows, k * cols : (k + 1) * cols]
                    term = piece * member(weights, m, first + c)
                    sums[c] = sums[c] + term if c in sums else term
                for c, total in sums.items():
                    at = first + c
                    if h:
                        total = total + sum_ref[r, at]
                    if r == 1 and h == folds - 1:
                        out_ref[at] = total
                        continue
                    sum_ref[r, at] = total
                    if h == folds - 1:
                        scale_ref[r // 2, at : at + 1, :] = jnp.max(jnp.abs(total), axis=0, keepdims=True)

    def send(unit):
        first, last = planes.place(unit[0])[0], planes.place(unit[-1])[0] + per
        for side, ref in enumerate((out_a_ref, out_b_ref)):
            level = code_of(scale_ref[side, first:last, :])
            scale_ref[side, first:last, :] = level
            factor = STEPS * scale_of(-level)
            for c in range(first, last):
                total = sum_ref[2 * side, c] * factor[c - first : c - first + 1]
                ref[c] = to_int16(jnp.floor(total + 0.5))

    planes.stages(unit, along_lat, send)
    for side, ref in enumerate((out_a_ref, out_b_ref)):
        for n in range(channels, ref.shape[0]):
            at = pl.ds((n - channels) * rows, rows)
            ref[n] = to_int16(scale_ref[side, at, :])


def code_of(largest):
    return jnp.ceil(jnp.log2(jnp.maximum(largest, 1e-36)) * 64.0)


def scale_of(level):
    return jnp.exp2(level * (1.0 / 64.0))


def to_int16(v):
    return v.astype(jnp.int32).astype(jnp.int16)


def add_kernel(total, out_ref, a_ref, b_ref, sum_ref, scale_ref):
    channels, rows, _ = out_ref.shape
    for side, ref in enumerate((a_ref, b_ref)):
        for n in range(channels, ref.shape[0]):
            at = pl.ds((n - channels) * rows, rows)
            scale_ref[side, at, :] = scale_of(ref[n].astype(F32)) * (1.0 / STEPS)
    for c in range(channels):
        added = out_ref[c]
        for side, ref in enumerate((a_ref, b_ref)):
            added = added + ref[c].astype(F32) * scale_ref[side, c : c + 1, :]
        sum_ref[c] = added / total


def call(kernel, out_shape, scratch_shapes=(), smem=0):
    def run(*args):
        n = len(args) - smem
        return pl.pallas_call(
            kernel,
            out_shape=out_shape,
            in_specs=whole(n) + [pl.BlockSpec(memory_space=pltpu.SMEM)] * smem,
            out_specs=whole(len(out_shape)) if isinstance(out_shape, tuple) else whole(1)[0],
            scratch_shapes=scratch_shapes,
            compiler_params=pltpu.CompilerParams(vmem_limit_bytes=GRANT),
        )(*args)

    return run


def inner_call(strips, slots, channels, members, rows, cols, parts):
    high = channels * members * rows
    return call(
        functools.partial(inner_kernel, slots, UNIT, parts),
        (jax.ShapeDtypeStruct((high, cols), F32), strips, strips),
        [pltpu.VMEM((high, cols), F32)],
    )


def outer_call(strip, slots, channels, members, rows, cols):
    high = channels * members * rows
    return call(
        functools.partial(outer_kernel, strip, slots, UNIT, members),
        jax.ShapeDtypeStruct((high, cols), F32),
        [pltpu.VMEM((2 * channels * members // slots * rows, LANES), F32)],
    )


def spread_call(slots, channels, members, rows, cols, parts):
    extra = -(-channels // rows)
    side = jax.ShapeDtypeStruct((channels + extra, rows, cols), jnp.int16)
    return call(
        functools.partial(spread_kernel, slots, UNIT, parts),
        (side, jax.ShapeDtypeStruct((channels, rows, cols), F32), side),
        [
            pltpu.VMEM((3, channels, rows, cols), F32),
            pltpu.VMEM((2, extra * rows, cols), F32),
        ],
    )


def add_call(total, channels, rows, cols):
    return call(
        functools.partial(add_kernel, total),
        jax.ShapeDtypeStruct((channels, rows, cols), F32),
        [pltpu.VMEM((2, -(-channels // rows) * rows, cols), F32)],
    )


def partners(count, first, closed):
    pairs = [(i, (i + 1) % count) for i in range(first, count if closed else count - 1, 2)]
    return sorted(set(pairs + [(j, i) for i, j in pairs]))


def local(grad_tokens, token_index, members, lat_taps, lon_taps):
    ens, lat_count, lon_count = (lax.axis_size(a) for a in ("ens", "lat", "lon"))
    ens_pos = lax.axis_index("ens")
    channels, cells = grad_tokens.shape
    rows, cols = token_index.shape
    own_channels = channels // ens
    blocks = lat_count * lon_count
    piece = cells // blocks
    strip = lon_taps.shape[0] - 1
    slots = LANES // strip
    assert cols == LANES and lon_count % 2 == 0 and lat_taps.shape[0] - 1 <= rows

    tokens = lax.dynamic_slice_in_dim(grad_tokens, ens_pos * own_channels, own_channels, 0)
    tokens = tokens.reshape(own_channels, blocks, piece).transpose(1, 0, 2)
    moved = lax.all_to_all(tokens, ("lat", "lon"), split_axis=0, concat_axis=0, tiled=True)
    if piece != LANES:
        moved = moved.transpose(1, 0, 2).reshape(own_channels, cells // LANES, LANES).transpose(1, 0, 2)

    lat_a, lat_b = partners(lat_count, 0, False), partners(lat_count, 1, False)
    lon_a, lon_b = partners(lon_count, 0, True), partners(lon_count, 1, True)
    if ens == 2:
        given = lax.dynamic_slice_in_dim(members, (1 - ens_pos) * own_channels, own_channels, 1)
        kept = lax.dynamic_slice_in_dim(members, ens_pos * own_channels, own_channels, 1)
        taken = lax.ppermute(given, "ens", [(0, 1), (1, 0)])
        w = [kept, taken]
    else:
        w = [lax.all_to_all(members, "ens", split_axis=1, concat_axis=0, tiled=True)]
    w_a, w_b = [], []
    for block in w:
        w_b.append(lax.ppermute(block, "lat", lat_b))
        w_a.append(lax.ppermute(block, "lat", lat_a))
    count = len(w) * w[0].shape[0]
    per = max(1, slots // count)

    strips = jax.ShapeDtypeStruct((max(1, count // slots), own_channels // per, rows, LANES), BF16)
    strip_a, strip_b, offset = pl.pallas_call(
        functools.partial(pack_kernel, strip, slots, len(w), lon_count, piece),
        out_shape=(strips, strips, jax.ShapeDtypeStruct((rows, cols), jnp.int32)),
        in_specs=whole(len(w)) + [pl.BlockSpec(memory_space=pl.ANY)], out_specs=whole(3), name="pack",
        scratch_shapes=[pltpu.VMEM((rows, cols), jnp.int32), pltpu.SemaphoreType.DMA],
        compiler_params=pltpu.CompilerParams(vmem_limit_bytes=GRANT),
    )(*w, token_index)
    matrix, edge_matrix = call(
        functools.partial(matrix_kernel, strip, lat_count, rows),
        (
            jax.ShapeDtypeStruct((3 * cols + 3 * rows, cols), BF16),
            jax.ShapeDtypeStruct((3 * LANES, slots // 2 * cols), BF16),
        ),
        smem=2,
    )(lat_taps, lon_taps)
    strip_b = lax.ppermute(strip_b, "lon", lon_b)
    strip_a = lax.ppermute(strip_a, "lon", lon_a)

    padded = -(-own_channels // slots) * slots
    edges = jax.ShapeDtypeStruct((padded // slots, rows, LANES), BF16)
    grid, grid_a, grid_b = pl.pallas_call(
        functools.partial(gather_kernel, strip, slots),
        out_shape=(jax.ShapeDtypeStruct((own_channels, rows, cols), BF16), edges, edges),
        in_specs=whole(2), out_specs=whole(3),
        scratch_shapes=[
            pltpu.VMEM((padded, rows, cols), F32),
            pltpu.VMEM((cells // LANES * (-(-own_channels // 8) * 8), LANES), BF16),
        ], name="gather",
        compiler_params=pltpu.CompilerParams(vmem_limit_bytes=GRANT),
    )(moved, offset)
    grid_b = lax.ppermute(grid_b, "lon", lon_b)
    grid_a = lax.ppermute(grid_a, "lon", lon_a)

    sizes = (own_channels, count, rows, cols, len(w))
    part, strip_a, strip_b = inner_call(strips, slots, *sizes)(*w, grid, matrix, strip_a, strip_b)
    mid = outer_call(strip, slots, *sizes[:4])(strip_a, strip_b, grid_a, grid_b, edge_matrix, part)
    out_a, out, out_b = spread_call(slots, *sizes)(*w, *w_a, *w_b, matrix, mid)
    out_b = lax.ppermute(out_b, "lat", lat_b)
    out_a = lax.ppermute(out_a, "lat", lat_a)
    return add_call(count - 1, own_channels, rows, cols)(out, out_a, out_b)


def solution(mesh):
    in_specs = (P(None, ("lat", "lon")), P("lat", "lon"), P("ens", None, "lat", "lon"), P(), P())
    out_specs = P("ens", "lat", "lon")

    return jax.shard_map(local, mesh=mesh, in_specs=in_specs, out_specs=out_specs, check_vma=False)
```

```python
import functools

import jax
import jax.numpy as jnp
from jax import lax
from jax.experimental import pallas as pl
from jax.experimental.pallas import tpu as pltpu
from jax.sharding import PartitionSpec as P


LANES = 128
F32 = jnp.float32
BF16 = jnp.bfloat16
UNIT = 7
STEPS = 32760.0
GRANT = 8 << 20


def whole(n):
    return [pl.BlockSpec(memory_space=pltpu.VMEM)] * n


def dot(a, b):
    return lax.dot_general(a, b, (((1,), (0,)), ((), ())), preferred_element_type=F32)


def split(v):
    hi = v.astype(BF16)
    return hi, (v - hi.astype(F32)).astype(BF16)


def band(taps, offset):
    total = jnp.zeros(offset.shape, F32)
    for k, tap in enumerate(taps):
        total = jnp.where(offset == k, tap, total)
    return total


def matrix_kernel(strip, lat_count, rows, lat_taps_ref, lon_taps_ref, matrix_ref, edge_ref):
    cols = matrix_ref.shape[1]
    count = lon_taps_ref.shape[0]
    iota = lax.broadcasted_iota
    taps = [lon_taps_ref[k] for k in range(count)]
    half = [sum(taps[a] * taps[a - d] for a in range(d, count)) for d in range(count)]
    both = half[:0:-1] + half
    place = iota(jnp.int32, (2 * LANES, cols), 0)
    inner = place % strip
    even = lax.rem(lax.axis_index("lon"), 2) == 0
    after = (place < cols + LANES // 2) == even
    source = jnp.where(place < cols, place, jnp.where(after, cols + inner, inner - strip))
    hi, lo = split(band(both, source - iota(jnp.int32, (2 * LANES, cols), 1) + count - 1))
    matrix_ref[: 3 * cols, :] = jnp.concatenate([hi[:cols], lo[:cols], hi[:cols]], axis=0)
    slot = iota(jnp.int32, (LANES, cols), 0) % (LANES // 2) // strip
    for k in range(LANES // 2 // strip):
        one, two = (jnp.where(slot == k, v[cols:], jnp.zeros_like(v[cols:])) for v in (hi, lo))
        edge_ref[:, k * cols : (k + 1) * cols] = jnp.concatenate([one, two, one], axis=0)
    count = lat_taps_ref.shape[0]
    radius = (count - 1) // 2
    taps = [lat_taps_ref[k] for k in range(count)]
    middle = rows + 2 * radius
    toward = jnp.where(lax.rem(lax.axis_index("lat"), 2) == 0, rows, -rows)
    place = iota(jnp.int32, (3 * rows, middle), 0)
    out_row = place % rows + (1 - place // rows) * toward
    mid_row = iota(jnp.int32, (3 * rows, middle), 1) - radius
    spread = band(taps, mid_row - out_row + radius)
    mid_row = iota(jnp.int32, (middle, rows), 0) - radius
    gather = band(taps[::-1], iota(jnp.int32, (middle, rows), 1) - mid_row + radius)
    whole_row = lax.axis_index("lat") * rows + mid_row
    gather = jnp.where((whole_row >= 0) & (whole_row < lat_count * rows), gather, 0.0)
    hi, lo = split(jnp.dot(spread, gather, precision=lax.Precision.HIGHEST, preferred_element_type=F32))
    matrix_ref[3 * cols :, : 3 * rows] = jnp.concatenate([hi, lo, hi], axis=1)


def pick_matrix(slot, strip, cols):
    even = lax.rem(lax.axis_index("lon"), 2) == 0
    last = cols - strip
    lane = lax.broadcasted_iota(jnp.int32, (cols, 2 * LANES), 1)
    row = lax.broadcasted_iota(jnp.int32, (cols, 2 * LANES), 0)
    first = jnp.where((lane < LANES) == even, last, 0)
    chosen = (lane % LANES // strip == slot) & (row == first + lane % strip)
    return jnp.where(chosen, 1.0, 0.0).astype(BF16)


def pack_kernel(strip, slots, parts, lon_count, piece, *refs):
    w_refs, (index_ref, a_ref, b_ref, offset_ref, landed, sem) = refs[:parts], refs[parts:]
    copy = pltpu.make_async_copy(index_ref, landed, sem)
    copy.start()
    each, channels, rows, cols = w_refs[0].shape
    members = each * parts
    per = max(1, slots // members)
    for h in range(max(1, members // slots)):
        total = None
        for k in range(slots):
            c2, m = (k // members, k % members) if members <= slots else (0, h * slots + k)
            plane = w_refs[m // each][m % each].reshape(channels // per, per, rows, cols)[:, c2]
            part = dot(plane.reshape(-1, cols), pick_matrix(k, strip, cols))
            total = part if total is None else total + part
        total = total.astype(BF16)
        a_ref[h] = total[:, :LANES].reshape(channels // per, rows, LANES)
        b_ref[h] = total[:, LANES:].reshape(channels // per, rows, LANES)
    copy.wait()
    cells = rows * cols
    block = lax.axis_index("lat") * lon_count + lax.axis_index("lon")
    index = landed[...]
    offset_ref[...] = lax.div(index, cells) * piece + lax.rem(index, cells) - block * piece


def gather_kernel(strip, slots, moved_ref, offset_ref, grid_ref, a_ref, b_ref, scratch, stack):
    pieces, channels, width = moved_ref.shape
    rows, cols = offset_ref.shape
    offset = offset_ref[...]
    scratch[channels:] = jnp.zeros((scratch.shape[0] - channels, rows, cols), F32)
    high = -(-channels // 8) * 8
    for n in range(pieces):
        stack[n * high : n * high + channels, :] = moved_ref[n]
    place = lax.broadcasted_iota(jnp.int32, (width, 2 * cols), 0)
    many = next(n for n in (16, 8, 4, 2, 1) if pieces % n == 0)
    for i in range(0, rows, 2):
        wanted = jnp.concatenate([offset[i : i + 1], offset[i + 1 : i + 2]], axis=1)
        chosen = jnp.where(place == lax.rem(wanted, width), 1.0, 0.0).astype(BF16)
        source = jnp.broadcast_to(lax.div(wanted, width), (high, 2 * cols))
        found = jnp.zeros((high, 2 * cols), F32)
        for n in range(0, pieces, many):
            some = dot(stack[n * high : (n + many) * high, :], chosen)
            for q in range(many):
                found = jnp.where(source == n + q, some[q * high : (q + 1) * high], found)
        scratch[:channels, i, :] = found[:channels, :cols]
        scratch[:channels, i + 1, :] = found[:channels, cols:]
    grid = scratch[...].astype(BF16)
    grid_ref[...] = grid[:channels]
    groups = scratch.shape[0] // slots
    planes = grid.reshape(groups, slots, rows, cols)
    total = None
    for k in range(slots):
        part = dot(planes[:, k].reshape(-1, cols), pick_matrix(k, strip, cols))
        total = part if total is None else total + part
    total = total.astype(BF16)
    a_ref[...] = total[:, :LANES].reshape(groups, rows, LANES)
    b_ref[...] = total[:, LANES:].reshape(groups, rows, LANES)


class Planes:
    def __init__(self, slots, members, channels):
        self.slots, self.members = slots, members
        self.per, self.folds = max(1, slots // members), max(1, members // slots)
        self.groups = channels // self.per * self.folds

    def place(self, n):
        first, h = n // self.folds * self.per, n % self.folds
        if self.folds == 1:
            return first, h, [(k // self.members, k % self.members) for k in range(self.slots)]
        return first, h, [(0, h * self.slots + k) for k in range(self.slots)]

    def stages(self, unit, *steps):
        units = [range(n, min(n + unit, self.groups)) for n in range(0, self.groups, unit)]
        for n in range(len(units) + len(steps) - 1):
            for behind, step in enumerate(steps):
                if 0 <= n - behind < len(units):
                    step(units[n - behind])


def member(refs, m, c):
    each = refs[0].shape[0]
    return refs[m // each][m % each, c].astype(F32)


def inner_kernel(slots, unit, parts, *refs):
    own_refs = refs[:parts]
    grid_ref, matrix_ref, strip_a_ref, strip_b_ref, part_ref, near_a_ref, near_b_ref, product_ref = refs[parts:]
    near_a_ref[...], near_b_ref[...] = strip_a_ref[...], strip_b_ref[...]
    each, channels, rows, cols = own_refs[0].shape
    planes = Planes(slots, each * parts, channels)
    height = slots * rows

    def weigh(unit):
        for n in unit:
            first, _, where = planes.place(n)
            for k, (c, m) in enumerate(where):
                at = pl.ds(n * height + k * rows, rows)
                product_ref[at, :] = member(own_refs, m, first + c) * grid_ref[first + c].astype(F32)

    def along_lon(unit):
        at = pl.ds(unit[0] * height, len(unit) * height)
        hi, lo = split(product_ref[at, :])
        part_ref[at, :] = dot(jnp.concatenate([hi, hi, lo], axis=1), matrix_ref[: 3 * cols, :])

    planes.stages(unit, weigh, along_lon)


def outer_kernel(
    strip, slots, unit, members, strip_a_ref, strip_b_ref, grid_a_ref, grid_b_ref, edge_ref, part_ref,
    mid_ref, side_ref,
):
    cols = part_ref.shape[1]
    folds, pairs, rows, _ = strip_a_ref.shape
    planes = Planes(slots, members, pairs * max(1, slots // members))
    per = planes.per
    half = LANES // 2
    src = lax.broadcasted_iota(jnp.int32, (LANES, LANES), 0)
    dst = lax.broadcasted_iota(jnp.int32, (LANES, LANES), 1)
    dst_channel = dst // strip // members if folds == 1 else jnp.zeros_like(dst)
    lane = lax.broadcasted_iota(jnp.int32, (rows, LANES), 1)
    low = lane < half
    expands = {}

    def weigh(unit):
        for n in unit:
            first, h, _ = planes.place(n)
            if first % slots not in expands:
                expand = src == ((first + dst_channel) % slots) * strip + dst % strip
                expands[first % slots] = jnp.where(expand, 1.0, 0.0).astype(BF16)
            expand = expands[first % slots]
            edge_a = strip_a_ref[h, first // per].astype(F32) * dot(grid_a_ref[first // slots], expand)
            edge_b = strip_b_ref[h, first // per].astype(F32) * dot(grid_b_ref[first // slots], expand)
            side_ref[pl.ds(2 * n * rows, rows), :] = jnp.where(low, edge_a, pltpu.roll(edge_b, half, 1))
            side_ref[pl.ds((2 * n + 1) * rows, rows), :] = jnp.where(low, pltpu.roll(edge_a, half, 1), edge_b)

    def along_lon(unit):
        hi, lo = split(side_ref[pl.ds(2 * unit[0] * rows, 2 * len(unit) * rows), :])
        found = dot(jnp.concatenate([hi, hi, lo], axis=1), edge_ref[...])
        for n in range(2 * len(unit)):
            for k in range(slots // 2):
                at = pl.ds(((2 * unit[0] + n) * (slots // 2) + k) * rows, rows)
                piece = found[n * rows : (n + 1) * rows, k * cols : (k + 1) * cols]
                mid_ref[at, :] = part_ref[at, :] + piece

    planes.stages(unit, weigh, along_lon)


def spread_kernel(slots, unit, parts, *refs):
    own_refs, a_refs, b_refs = (refs[n * parts : (n + 1) * parts] for n in range(3))
    matrix_ref, mid_ref, out_a_ref, out_ref, out_b_ref, sum_ref, scale_ref = refs[3 * parts :]
    each, channels, rows, cols = own_refs[0].shape
    planes = Planes(slots, each * parts, channels)
    per, folds = planes.per, planes.folds
    height = slots * rows
    scale_ref[...] = jnp.zeros_like(scale_ref)

    def along_lat(unit):
        for n in unit:
            first, h, where = planes.place(n)
            hi, lo = split(mid_ref[pl.ds(n * height, height), :])
            stack = []
            for k in range(slots):
                at = slice(k * rows, (k + 1) * rows)
                stack.append(jnp.concatenate([hi[at], hi[at], lo[at]], axis=0))
            spread = dot(matrix_ref[3 * cols :, : 3 * rows], jnp.concatenate(stack, axis=1))
            for r, weights in enumerate((a_refs, own_refs, b_refs)):
                sums = {}
                for k, (c, m) in enumerate(where):
                    piece = spread[r * rows : (r + 1) * rows, k * cols : (k + 1) * cols]
                    term = piece * member(weights, m, first + c)
                    sums[c] = sums[c] + term if c in sums else term
                for c, total in sums.items():
                    at = first + c
                    if h:
                        total = total + sum_ref[r, at]
                    if r == 1 and h == folds - 1:
                        out_ref[at] = total
                        continue
                    sum_ref[r, at] = total
                    if h == folds - 1:
                        scale_ref[r // 2, at : at + 1, :] = jnp.max(jnp.abs(total), axis=0, keepdims=True)

    def send(unit):
        first, last = planes.place(unit[0])[0], planes.place(unit[-1])[0] + per
        for side, ref in enumerate((out_a_ref, out_b_ref)):
            level = code_of(scale_ref[side, first:last, :])
            scale_ref[side, first:last, :] = level
            factor = STEPS * scale_of(-level)
            for c in range(first, last):
                total = sum_ref[2 * side, c] * factor[c - first : c - first + 1]
                ref[c] = to_int16(jnp.floor(total + 0.5))

    planes.stages(unit, along_lat, send)
    for side, ref in enumerate((out_a_ref, out_b_ref)):
        for n in range(channels, ref.shape[0]):
            at = pl.ds((n - channels) * rows, rows)
            ref[n] = to_int16(scale_ref[side, at, :])


def code_of(largest):
    return jnp.ceil(jnp.log2(jnp.maximum(largest, 1e-36)) * 64.0)


def scale_of(level):
    return jnp.exp2(level * (1.0 / 64.0))


def to_int16(v):
    return v.astype(jnp.int32).astype(jnp.int16)


def add_kernel(total, out_ref, a_ref, b_ref, result_ref, sum_ref, scale_ref, sems):
    channels, rows, _ = out_ref.shape
    size, copies = channels // sems.shape[0], []
    for side, ref in enumerate((a_ref, b_ref)):
        for n in range(channels, ref.shape[0]):
            at = pl.ds((n - channels) * rows, rows)
            scale_ref[side, at, :] = scale_of(ref[n].astype(F32)) * (1.0 / STEPS)
    for c in range(channels):
        added = out_ref[c]
        for side, ref in enumerate((a_ref, b_ref)):
            added = added + ref[c].astype(F32) * scale_ref[side, c : c + 1, :]
        sum_ref[c] = added / total
        if (c + 1) % size == 0:
            at = pl.ds(c + 1 - size, size)
            copies.append(pltpu.make_async_copy(sum_ref.at[at], result_ref.at[at], sems.at[c // size]))
            copies[-1].start()
    for copy in copies:
        copy.wait()


def call(kernel, out_shape, scratch_shapes=(), smem=0):
    def run(*args):
        n = len(args) - smem
        return pl.pallas_call(
            kernel,
            out_shape=out_shape,
            in_specs=whole(n) + [pl.BlockSpec(memory_space=pltpu.SMEM)] * smem,
            out_specs=whole(len(out_shape)) if isinstance(out_shape, tuple) else whole(1)[0],
            scratch_shapes=scratch_shapes,
            compiler_params=pltpu.CompilerParams(vmem_limit_bytes=GRANT),
        )(*args)

    return run


def inner_call(strips, slots, channels, members, rows, cols, parts):
    high = channels * members * rows
    return call(
        functools.partial(inner_kernel, slots, UNIT, parts),
        (jax.ShapeDtypeStruct((high, cols), F32), strips, strips),
        [pltpu.VMEM((high, cols), F32)],
    )


def outer_call(strip, slots, channels, members, rows, cols):
    high = channels * members * rows
    return call(
        functools.partial(outer_kernel, strip, slots, UNIT, members),
        jax.ShapeDtypeStruct((high, cols), F32),
        [pltpu.VMEM((2 * channels * members // slots * rows, LANES), F32)],
    )


def spread_call(slots, channels, members, rows, cols, parts):
    extra = -(-channels // rows)
    side = jax.ShapeDtypeStruct((channels + extra, rows, cols), jnp.int16)
    return call(
        functools.partial(spread_kernel, slots, UNIT, parts),
        (side, jax.ShapeDtypeStruct((channels, rows, cols), F32), side),
        [
            pltpu.VMEM((3, channels, rows, cols), F32),
            pltpu.VMEM((2, extra * rows, cols), F32),
        ],
    )


def add_call(total, channels, rows, cols):
    block = jax.ShapeDtypeStruct((channels, rows, cols), F32)
    chunks = 4 if channels % 4 == 0 else 1
    return pl.pallas_call(
        functools.partial(add_kernel, total),
        out_shape=block, in_specs=whole(3), out_specs=pl.BlockSpec(memory_space=pl.ANY), name="add",
        scratch_shapes=[
            pltpu.VMEM((channels, rows, cols), F32),
            pltpu.VMEM((2, -(-channels // rows) * rows, cols), F32),
            pltpu.SemaphoreType.DMA((chunks,)),
        ],
        compiler_params=pltpu.CompilerParams(vmem_limit_bytes=GRANT),
    )


def partners(count, first, closed):
    pairs = [(i, (i + 1) % count) for i in range(first, count if closed else count - 1, 2)]
    return sorted(set(pairs + [(j, i) for i, j in pairs]))


def local(grad_tokens, token_index, members, lat_taps, lon_taps):
    ens, lat_count, lon_count = (lax.axis_size(a) for a in ("ens", "lat", "lon"))
    ens_pos = lax.axis_index("ens")
    channels, cells = grad_tokens.shape
    rows, cols = token_index.shape
    own_channels = channels // ens
    blocks = lat_count * lon_count
    piece = cells // blocks
    strip = lon_taps.shape[0] - 1
    slots = LANES // strip
    assert cols == LANES and lon_count % 2 == 0 and lat_taps.shape[0] - 1 <= rows

    tokens = lax.dynamic_slice_in_dim(grad_tokens, ens_pos * own_channels, own_channels, 0)
    tokens = tokens.reshape(own_channels, blocks, piece).transpose(1, 0, 2)
    moved = lax.all_to_all(tokens, ("lat", "lon"), split_axis=0, concat_axis=0, tiled=True)
    if piece != LANES:
        moved = moved.transpose(1, 0, 2).reshape(own_channels, cells // LANES, LANES).transpose(1, 0, 2)

    lat_a, lat_b = partners(lat_count, 0, False), partners(lat_count, 1, False)
    lon_a, lon_b = partners(lon_count, 0, True), partners(lon_count, 1, True)
    if ens == 2:
        given = lax.dynamic_slice_in_dim(members, (1 - ens_pos) * own_channels, own_channels, 1)
        kept = lax.dynamic_slice_in_dim(members, ens_pos * own_channels, own_channels, 1)
        taken = lax.ppermute(given, "ens", [(0, 1), (1, 0)])
        w = [kept, taken]
    else:
        w = [lax.all_to_all(members, "ens", split_axis=1, concat_axis=0, tiled=True)]
    w_a, w_b = [], []
    for block in w:
        w_b.append(lax.ppermute(block, "lat", lat_b))
        w_a.append(lax.ppermute(block, "lat", lat_a))
    count = len(w) * w[0].shape[0]
    per = max(1, slots // count)

    strips = jax.ShapeDtypeStruct((max(1, count // slots), own_channels // per, rows, LANES), BF16)
    strip_a, strip_b, offset = pl.pallas_call(
        functools.partial(pack_kernel, strip, slots, len(w), lon_count, piece),
        out_shape=(strips, strips, jax.ShapeDtypeStruct((rows, cols), jnp.int32)),
        in_specs=whole(len(w)) + [pl.BlockSpec(memory_space=pl.ANY)], out_specs=whole(3), name="pack",
        scratch_shapes=[pltpu.VMEM((rows, cols), jnp.int32), pltpu.SemaphoreType.DMA],
        compiler_params=pltpu.CompilerParams(vmem_limit_bytes=GRANT),
    )(*w, token_index)
    matrix, edge_matrix = call(
        functools.partial(matrix_kernel, strip, lat_count, rows),
        (
            jax.ShapeDtypeStruct((3 * cols + 3 * rows, cols), BF16),
            jax.ShapeDtypeStruct((3 * LANES, slots // 2 * cols), BF16),
        ),
        smem=2,
    )(lat_taps, lon_taps)
    strip_b = lax.ppermute(strip_b, "lon", lon_b)
    strip_a = lax.ppermute(strip_a, "lon", lon_a)

    padded = -(-own_channels // slots) * slots
    edges = jax.ShapeDtypeStruct((padded // slots, rows, LANES), BF16)
    grid, grid_a, grid_b = pl.pallas_call(
        functools.partial(gather_kernel, strip, slots),
        out_shape=(jax.ShapeDtypeStruct((own_channels, rows, cols), BF16), edges, edges),
        in_specs=whole(2), out_specs=whole(3),
        scratch_shapes=[
            pltpu.VMEM((padded, rows, cols), F32),
            pltpu.VMEM((cells // LANES * (-(-own_channels // 8) * 8), LANES), BF16),
        ], name="gather",
        compiler_params=pltpu.CompilerParams(vmem_limit_bytes=GRANT),
    )(moved, offset)
    grid_b = lax.ppermute(grid_b, "lon", lon_b)
    grid_a = lax.ppermute(grid_a, "lon", lon_a)

    sizes = (own_channels, count, rows, cols, len(w))
    part, strip_a, strip_b = inner_call(strips, slots, *sizes)(*w, grid, matrix, strip_a, strip_b)
    mid = outer_call(strip, slots, *sizes[:4])(strip_a, strip_b, grid_a, grid_b, edge_matrix, part)
    out_a, out, out_b = spread_call(slots, *sizes)(*w, *w_a, *w_b, matrix, mid)
    out_b = lax.ppermute(out_b, "lat", lat_b)
    out_a = lax.ppermute(out_a, "lat", lat_a)
    return add_call(count - 1, own_channels, rows, cols)(out, out_a, out_b)


def solution(mesh):
    in_specs = (P(None, ("lat", "lon")), P("lat", "lon"), P("ens", None, "lat", "lon"), P(), P())
    out_specs = P("ens", "lat", "lon")

    return jax.shard_map(local, mesh=mesh, in_specs=in_specs, out_specs=out_specs, check_vma=False)
```
